32 devices in a mesh: mesh: 8 (over z, core), run: 4 (over y, x).
Axes of the slice: x: 2, y: 2, z: 4, core: 2. Of those that a mesh axis runs over, the one named last changes fastest.
Arguments:
- snapshots: bfloat16 [16384, 2048], P('mesh', 'run'), may hold values from -6 to 6
- block_cols: int32 [256, 16], P('mesh'), may hold values from 0 to 255, as said below
- mass_blocks: bfloat16 [256, 64, 1024], P('mesh'), as said below
Outputs:
- gram: float32 [2048, 2048], P('mesh', 'run')
The draws below stay inside these ranges and needn't reach their ends.
Inputs may be any that keep to these rules, and one draw needn't show every extreme that they name: `block_cols`: block row b names 16 different block columns, the first of them b itself; all lie from 2 blocks before the first block row of shard b // 32 to 2 blocks after its last. In every shard but the first, its first block row names the block 2 before the shard; in every shard but the last, its last block row names the block 2 after it. `mass_blocks`: entry [b, i, k * 64 + j] is row i, column j of the k-th stored block of block row b, in the order of block_cols.
All inputs are finite; a program needn't handle non-finite values.
Results may differ from the reference program's by a relative error of at most 0.00056.
Values may be sent and summed in bfloat16 or wider, within the bound.
No kernel may reach another device: no remote copies, remote signals or barrier semaphores. Data moves between devices by JAX's collectives and lax.ppermute only.
A program may use at most 128 MiB of HBM per device.

```python
import math
import jax
import jax.numpy as jnp
from jax import lax

SNAP = 2048
BLK = 64
KB = 16
HB = 2
NB = 32
NBLK = 256
NODES = 16384
N_MESH = 8


def draw_block_cols(key, part):
    window_size = NB + 2 * HB
    position = jnp.arange(window_size, dtype=jnp.int32)[None, :]
    block_rows = jnp.arange(NBLK, dtype=jnp.int32)[:, None]
    shard_index = block_rows // NB
    inner_row = block_rows % NB
    global_cols = shard_index * NB - HB + position
    inside = (global_cols >= 0) & (global_cols < NBLK)
    random_score = jax.random.randint(key, (NBLK, window_size), 0, 2 ** 20, dtype=jnp.int32) * window_size + position
    forced_edge = (inner_row == 0) & (position == 0) | (inner_row == NB - 1) & (position == window_size - 1)
    scores = jnp.where(inside, random_score, -1 - position)
    scores = jnp.where(forced_edge & inside, 2 ** 29, scores)
    scores = jnp.where(position == inner_row + HB, 2 ** 30, scores)
    best_scores, chosen = lax.top_k(scores, KB)
    return (shard_index * NB - HB + chosen.astype(jnp.int32)).astype(jnp.int32)


def draw_mass_blocks(key, part):
    key_off = jax.random.fold_in(key, 11)
    key_diag = jax.random.fold_in(key, 23)
    off_blocks = jax.random.normal(key_off, (NBLK, KB, BLK, BLK), jnp.float32) * (0.5 / math.sqrt(KB * BLK))
    diagonal = jax.random.uniform(key_diag, (NBLK, BLK), jnp.float32, 0.5, 2.0)
    identity = jnp.eye(BLK, dtype=jnp.float32)
    first_slot = (jnp.arange(KB) == 0).astype(jnp.float32)
    assembled = off_blocks + first_slot[None, :, None, None] * identity[None, None] * diagonal[:, None, :, None]
    arranged = jnp.transpose(assembled, (0, 2, 1, 3)).reshape(NBLK, BLK, KB * BLK)
    return (arranged / NODES).astype(jnp.bfloat16)


def raised(entries, stream_key, source, target, parts, factor):
    owner, partner = [(jnp.arange(entries.shape[axis_at]) // (entries.shape[axis_at] // parts)).reshape([-1 if axis == axis_at else 1 for axis in range(entries.ndim)]) for axis_at in (source, target)]
    chosen = jax.random.permutation(stream_key, parts)[partner]
    strong = (owner == chosen) | (owner == (partner + parts // 2) % parts)
    return jnp.where(strong, factor * entries, entries)


def block_levels(rng, dims, cuts, low, top_value):
    def one(dim, blocks):
        steps = jax.random.uniform(jax.random.fold_in(jax.random.fold_in(rng, 6), dim), (blocks,), jnp.float32, low / len(cuts), top_value / len(cuts))
        return jnp.repeat(jnp.exp(steps), dims[dim] // blocks).reshape((-1,) + (1,) * (len(dims) - dim - 1))

    gain = one(*cuts[0])
    for cut in cuts[1:]:
        gain = gain * one(*cut)
    return gain


def noise_with(rng, extent, scale, most, cuts, heavy, held_as=jnp.bfloat16):
    entries = scale * jax.random.normal(rng, extent, jnp.float32)
    if cuts:
        entries = entries * block_levels(rng, extent, cuts, -0.22, 0.18)
    return jnp.clip(raised(entries, jax.random.fold_in(rng, 3), *heavy), -most, most).astype(held_as)


def setup_inputs(seed: int = 0) -> dict:
    seeds = jax.random.split(jax.random.key(seed), 4)
    snapshots = noise_with(seeds[0], (NODES, SNAP), 1.0, 6.0, ((0, 8), (1, 4)), (0, 1, 8, 2.0))
    block_cols = draw_block_cols(jax.random.fold_in(seeds[3], 71), 0)
    mass_blocks = draw_mass_blocks(jax.random.fold_in(seeds[3], 71), 0)
    return dict(snapshots=snapshots, block_cols=block_cols, mass_blocks=mass_blocks)


def reference(snapshots, block_cols, mass_blocks):
    block_total = block_cols.shape[0]
    blocked = snapshots.reshape(block_total, BLK, SNAP)

    def one_shard(pieces):
        shard_cols, shard_mass = pieces
        picked = blocked[shard_cols].reshape(NB, KB * BLK, SNAP)
        products = jnp.einsum("bim,bmc->bic", shard_mass.astype(jnp.float32), picked.astype(jnp.float32))
        return products.astype(jnp.bfloat16)

    weighted = lax.map(one_shard, (block_cols.reshape(N_MESH, NB, KB), mass_blocks.reshape(N_MESH, NB, BLK, KB * BLK)))
    weighted = weighted.reshape(NODES, SNAP)
    return lax.dot_general(snapshots, weighted, (((0,), (0,)), ((), ())), preferred_element_type=jnp.float32)
```

```python
import functools

import jax
import jax.numpy as jnp
from jax import lax
from jax.experimental import pallas as pl
from jax.experimental.pallas import tpu as pltpu
from jax.sharding import PartitionSpec as P

HB = 2


def contract_nodes(left_cols, right_cols):
    return lax.dot_general(
        left_cols, right_cols, (((0,), (0,)), ((), ())), preferred_element_type=jnp.float32
    )


def weigh_body(places, group, blk, cols_ref, mass_ref, *refs):
    count = len(places)
    pieces, out_ref, rows_ref, sems = refs[:count], refs[count], refs[count + 1], refs[count + 2]
    step = pl.program_id(0)

    @pl.when(step == 0)
    def _():
        copies = [
            pltpu.make_async_copy(
                piece, rows_ref.at[r : r + piece.shape[0], c : c + piece.shape[1]], sems.at[i]
            )
            for i, (piece, (r, c)) in enumerate(zip(pieces, places))
        ]
        for copy in copies:
            copy.start()
        for copy in copies:
            copy.wait()

    for i in range(group):
        row = step * group + i
        picked = jnp.concatenate(
            [
                rows_ref[pl.ds(pl.multiple_of(cols_ref[row, k] * blk, blk), blk), :]
                for k in range(cols_ref.shape[1])
            ],
            axis=0,
        )
        product = jnp.dot(mass_ref[i], picked, preferred_element_type=jnp.float32)
        out_ref[i * blk : (i + 1) * blk, :] = product.astype(out_ref.dtype)


def weigh(local_cols, mass_blocks, pieces, places, width):
    block_rows, blk, stored = mass_blocks.shape
    group = next(g for g in (8, 4, 2, 1) if block_rows % g == 0)
    row_count = block_rows * blk + 2 * HB * blk
    spec = pltpu.PrefetchScalarGridSpec(
        num_scalar_prefetch=1,
        grid=(block_rows // group,),
        in_specs=[pl.BlockSpec((group, blk, stored), lambda g, cols: (g, 0, 0))]
        + [pl.BlockSpec(memory_space=pl.ANY)] * len(pieces),
        out_specs=pl.BlockSpec((group * blk, width), lambda g, cols: (g, 0)),
        scratch_shapes=[
            pltpu.VMEM((row_count, width), jnp.bfloat16),
            pltpu.SemaphoreType.DMA((len(pieces),)),
        ],
    )
    return pl.pallas_call(
        functools.partial(weigh_body, places, group, blk),
        grid_spec=spec,
        out_shape=jax.ShapeDtypeStruct((block_rows * blk, width), jnp.bfloat16),
        cost_estimate=pl.CostEstimate(
            flops=8 * block_rows * blk * stored * width,
            bytes_accessed=2 * (block_rows * blk * stored + 2 * row_count * width),
            transcendentals=0,
        ),
        name="weigh",
    )(local_cols, mass_blocks, *pieces)


def product_body(steps, pick_ref, *refs):
    keep_ref, send_ref, first_ref, second_ref = refs[-4:]
    left_a, left_b, w = refs[:3]
    extra = refs[3:5] if len(refs) == 9 else None
    step = pl.program_id(0)
    own = w.shape[1]

    def add(acc_ref, left, right, lo):
        part = contract_nodes(left[...], right[...])
        hi = lo + right.shape[1]

        @pl.when(step == 0)
        def _():
            acc_ref[:, lo:hi] = part

        @pl.when(step > 0)
        def _():
            acc_ref[:, lo:hi] += part

    add(first_ref, left_a, w, 0)
    add(second_ref, left_b, w, 0)
    if extra is not None:
        add(first_ref, left_a, extra[1], own)
        add(second_ref, left_b, extra[0], own)

    @pl.when((step == steps - 1) & (pick_ref[0] == 0))
    def _():
        keep_ref[...] = first_ref[...]
        send_ref[...] = second_ref[...]

    @pl.when((step == steps - 1) & (pick_ref[0] != 0))
    def _():
        keep_ref[...] = second_ref[...]
        send_ref[...] = first_ref[...]


def products(pick, left, w, extra=None):
    nodes, own = w.shape
    steps = next(s for s in (4, 2, 1) if nodes % s == 0)
    depth = nodes // steps
    if isinstance(left, tuple):
        width = left[0].shape[1]
        operands = [left[0], left[1], w]
        specs = [pl.BlockSpec((depth, width), lambda k, p: (k, 0))] * 2
    else:
        width = left.shape[1] // 2
        operands = [left, left, w]
        specs = [
            pl.BlockSpec((depth, width), lambda k, p: (k, 0)),
            pl.BlockSpec((depth, width), lambda k, p: (k, 1)),
        ]
    specs.append(pl.BlockSpec((depth, own), lambda k, p: (k, 0)))
    total = own
    if extra is not None:
        half = extra.shape[1] // 2
        total += half
        operands += [extra, extra]
        specs += [
            pl.BlockSpec((depth, half), lambda k, p: (k, 0)),
            pl.BlockSpec((depth, half), lambda k, p: (k, 1)),
        ]
    result = jax.ShapeDtypeStruct((width, total), jnp.float32)
    whole = pl.BlockSpec((width, total), lambda k, p: (0, 0))
    return pl.pallas_call(
        functools.partial(product_body, steps),
        grid_spec=pltpu.PrefetchScalarGridSpec(
            num_scalar_prefetch=1,
            grid=(steps,),
            in_specs=specs,
            out_specs=[whole, whole],
            scratch_shapes=[pltpu.VMEM((width, total), jnp.float32)] * 2,
        ),
        out_shape=[result, result],
        cost_estimate=pl.CostEstimate(
            flops=4 * nodes * width * total,
            bytes_accessed=2 * nodes * (2 * width + total) + 8 * width * total,
            transcendentals=0,
        ),
        name="products",
    )(pick, *operands)


LINE = {
    0: (((1, 0), (3, 2)), ((2, 0),)),
    1: (((0, 1), (3, 2)), ((2, 1),)),
    2: (((3, 2), (0, 1)), ((1, 2),)),
    3: (((2, 3), (0, 1)), ((1, 3),)),
}
X, Y = 1, 2


def everywhere(chips, runs):
    return [(z, c, q) for z in range(chips) for c in range(2) for q in range(runs)]


def exchange_plan(chips, runs):
    flat = lambda z, c, q: (2 * z + c) * runs + q
    across = lambda bit: [(q, q ^ bit) for q in range(runs)]
    cores = [(m, m ^ 1) for m in range(2 * chips)]

    def line(target, round_):
        return [
            (flat(s, c, q), flat(t, c, q))
            for c in range(2)
            for q in range(runs)
            for s, t in LINE[target(c, q)][round_]
        ]

    def corner(target, bit):
        return [
            (flat(target(c, q), c, q), flat(target(c, q), c, q ^ bit(c)))
            for c in range(2)
            for q in range(runs)
        ]

    return across, cores, line, corner


def on_square(snapshots, block_cols, mass_blocks):
    node_count, column_count = snapshots.shape
    blk = mass_blocks.shape[1]
    blocks_here = node_count // blk
    rim = HB * blk
    half = column_count // 2
    runs = lax.axis_size("run")
    chips = lax.axis_size("mesh") // 2
    both = ("mesh", "run")
    across, cores, line, corner = exchange_plan(chips, runs)
    shard = lax.axis_index("mesh")
    column = lax.axis_index("run")
    core, chip = shard % 2, shard // 2
    local_cols = block_cols - (shard * blocks_here - HB)

    def over_x(v):
        return lax.ppermute(v, "run", across(X))

    def over_y(v):
        return lax.ppermute(v, "run", across(Y))

    left, right = snapshots[:, :half], snapshots[:, half:]
    a1, b2 = over_x(left), over_y(right)
    shards = 2 * chips
    low = lax.ppermute(snapshots[-rim:], "mesh", [(i, i + 1) for i in range(shards - 1)])
    high = lax.ppermute(snapshots[:rim], "mesh", [(i + 1, i) for i in range(shards - 1)])
    rims = jnp.concatenate([low, high], axis=0)
    ra, rb = over_x(rims[:, :half]), over_y(rims[:, half:])
    left, right, ra, rb = lax.optimization_barrier((left, right, ra, rb))
    a2, b1 = over_x(right), over_y(left)

    top = rim + node_count
    w = weigh(
        local_cols, mass_blocks, [low, snapshots, high], [(0, 0), (rim, 0), (top, 0)], column_count
    )

    def summed(kept, sent, target):
        total = kept + lax.ppermute(sent, "mesh", cores)
        for round_ in range(2):
            total = total + lax.ppermute(total, both, line(target, round_))
        return total

    pick = core[None].astype(jnp.int32)
    own = summed(*products(pick, snapshots, w), lambda c, q: q)

    wx = weigh(
        local_cols,
        mass_blocks,
        [ra[:rim], a1, ra[rim:], rb[:rim], b2, rb[rim:]],
        [(0, 0), (rim, 0), (top, 0), (0, half), (rim, half), (top, half)],
        column_count,
    )

    def stage(a, b, core_a):
        pick_here = (core != core_a)[None].astype(jnp.int32)
        target = lambda c, q: q ^ (X if c == core_a else Y)
        total = summed(*products(pick_here, (a, b), w, wx), target)
        moved = lax.ppermute(
            total[:, column_count:], both, corner(target, lambda c: Y if c == core_a else X)
        )
        return total[:, :column_count], moved

    near1, far1 = stage(a1, b2, 0)
    near2, far2 = stage(a2, b1, 1)
    first = core == 0
    far = jnp.concatenate([jnp.where(first, far2, far1), jnp.where(first, far1, far2)], axis=1)
    near = jnp.where((chip == (column ^ X)) == first, near1, near2)
    return jnp.where(chip == column, own, jnp.where(chip == (column ^ (X | Y)), far, near))


def on_device(snapshots, block_cols, mass_blocks):
    node_count, column_count = snapshots.shape
    blk = mass_blocks.shape[1]
    blocks_here = node_count // blk
    rim = HB * blk
    shards = lax.axis_size("mesh")
    low = lax.ppermute(snapshots[-rim:], "mesh", [(i, i + 1) for i in range(shards - 1)])
    high = lax.ppermute(snapshots[:rim], "mesh", [(i + 1, i) for i in range(shards - 1)])
    local_cols = block_cols - (lax.axis_index("mesh") * blocks_here - HB)
    weighted = weigh(
        local_cols,
        mass_blocks,
        [low, snapshots, high],
        [(0, 0), (rim, 0), (rim + node_count, 0)],
        column_count,
    )
    gathered = lax.all_gather(snapshots, "run", axis=1, tiled=True)
    return lax.psum_scatter(
        contract_nodes(gathered, weighted), "mesh", scatter_dimension=0, tiled=True
    )


def solution(mesh):
    placed = (P("mesh", "run"), P("mesh", None), P("mesh", None, None))
    square = mesh.shape["run"] == 4 and mesh.shape["mesh"] == 8
    return jax.shard_map(
        on_square if square else on_device,
        mesh=mesh,
        in_specs=placed,
        out_specs=P("mesh", "run"),
        check_vma=False,
    )
```

```python
import functools

import jax
import jax.numpy as jnp
from jax import lax
from jax.experimental import pallas as pl
from jax.experimental.pallas import tpu as pltpu
from jax.sharding import PartitionSpec as P


HB = 2


def contract_nodes(left_cols, right_cols):
    return lax.dot_general(
        left_cols, right_cols, (((0,), (0,)), ((), ())), preferred_element_type=jnp.float32
    )


def span(start, size):
    return slice(start, start + size)


def fused_body(plan, *refs):
    refs = list(refs)
    cols_ref, pick_ref = refs.pop(0), refs.pop(0)
    mass_hbm = refs.pop(0) if plan["weighs"] else None
    pieces = [refs.pop(0) for _ in range(plan["count"])]
    own_hbm = refs.pop(0) if plan["own"] else None
    extra_hbm = refs.pop(0) if plan["extra"] else None
    made_ref = refs.pop(0) if plan["weighs"] else None
    keep_ref, send_ref = (refs.pop(0), refs.pop(0)) if plan["multiplies"] else (None, None)
    rows_ref = refs.pop(0)
    mass_ref = refs.pop(0) if plan["weighs"] else None
    own_ref = refs.pop(0) if plan["own"] else None
    extra_ref = refs.pop(0) if plan["extra"] else None
    sems = refs.pop(0)
    blk, rim, half = plan["blk"], plan["rim"], plan["half"]

    used = iter(range(64))
    fetch = lambda source, target: pltpu.make_async_copy(source, target, sems.at[next(used)])
    rows_in = [
        fetch(pieces[p].at[span(r, n), :], rows_ref.at[span(to, n), span(lane, pieces[p].shape[1])])
        for p, r, n, to, lane in plan["places"]
    ]
    mass_in, own_in, extra_in = [], [], []
    if plan["weighs"]:
        parts = plan["parts"]
        size = mass_ref.shape[0] // parts
        mass_in = [
            fetch(mass_hbm.at[span(i * size, size)], mass_ref.at[span(i * size, size)])
            for i in range(parts)
        ]
    if plan["own"]:
        own_in = [fetch(own_hbm, own_ref)]
    if plan["extra"]:
        extra_in = [fetch(extra_hbm, extra_ref)]
    for copy in rows_in + mass_in + own_in + extra_in:
        copy.start()
    for copy in rows_in:
        copy.wait()

    if plan["weighs"]:
        for row in range(mass_ref.shape[0]):
            if row % size == 0:
                mass_in[row // size].wait()
            picked = jnp.concatenate(
                [
                    rows_ref[pl.ds(pl.multiple_of(cols_ref[row, k] * blk, blk), blk), :]
                    for k in range(cols_ref.shape[1])
                ],
                axis=0,
            )
            product = jnp.dot(mass_ref[row], picked, preferred_element_type=jnp.float32)
            made_ref[row * blk : (row + 1) * blk, :] = product.astype(made_ref.dtype)
    for copy in own_in + extra_in:
        copy.wait()

    if plan["multiplies"]:
        w_ref = own_ref if plan["own"] else made_ref
        x_ref = extra_ref if plan["extra"] else (made_ref if plan["own"] else None)
        own = w_ref.shape[1]
        nodes = w_ref.shape[0]
        lead = rim if plan["padded"] else 0
        for target, first in ((keep_ref, pick_ref[0]), (send_ref, 1 - pick_ref[0])):
            left = rows_ref[span(lead, nodes), pl.ds(pl.multiple_of(first * half, half), half)]
            target[:, :own] = contract_nodes(left, w_ref[...])
            if x_ref is not None:
                right = x_ref[:, pl.ds(pl.multiple_of((1 - first) * half, half), half)]
                target[:, own:] = contract_nodes(left, right)


def fused(local_cols, pick, mass_blocks, pieces, places, own=None, extra=None, weighs=True, multiplies=True):
    block_rows, blk, stored = mass_blocks.shape
    rim = HB * blk
    nodes = block_rows * blk
    width = max(lane + pieces[p].shape[1] for p, _, _, _, lane in places)
    half = width // 2
    row_count = max(to + n for _, _, n, to, _ in places)
    parts = 4 if block_rows % 4 == 0 else 1
    plan = dict(
        blk=blk, rim=rim, half=half, weighs=weighs, multiplies=multiplies, places=places,
        count=len(pieces), own=own is not None, extra=extra is not None,
        padded=row_count > nodes, parts=parts,
    )
    total = width + half if own is not None else width
    operands, scratch = [], [pltpu.VMEM((row_count, width), jnp.bfloat16)]
    outs, flops = [], 0
    if weighs:
        operands.append(mass_blocks)
        scratch.append(pltpu.VMEM(mass_blocks.shape, jnp.bfloat16))
        outs.append(jax.ShapeDtypeStruct((nodes, width), jnp.bfloat16))
        flops += 8 * nodes * stored * width
    operands += pieces
    for w in (own, extra):
        if w is not None:
            operands.append(w)
            scratch.append(pltpu.VMEM(w.shape, jnp.bfloat16))
    if multiplies:
        outs += [jax.ShapeDtypeStruct((half, total), jnp.float32)] * 2
        flops += 4 * nodes * half * total
    scratch.append(pltpu.SemaphoreType.DMA((len(places) + parts + 2,)))
    return pl.pallas_call(
        functools.partial(fused_body, plan),
        grid_spec=pltpu.PrefetchScalarGridSpec(
            num_scalar_prefetch=2,
            grid=(),
            in_specs=[pl.BlockSpec(memory_space=pl.ANY)] * len(operands),
            out_specs=[pl.BlockSpec(memory_space=pltpu.VMEM)] * len(outs),
            scratch_shapes=scratch,
        ),
        out_shape=outs,
        cost_estimate=pl.CostEstimate(flops=flops, bytes_accessed=8 << 20, transcendentals=0),
    )(local_cols, pick, *operands)


TOP = 32000.0
EXTRA = 16


def encoded(values):
    peak = jnp.maximum(jnp.max(jnp.abs(values), axis=0, keepdims=True), 1e-30)
    power = jnp.ceil(jnp.log2(peak))
    whole = jnp.round(values * (jnp.exp2(-power) * TOP)).astype(jnp.int32)
    return whole.astype(jnp.int16), power.astype(jnp.int32)


def put_encoded(target, values):
    rows, width = values.shape
    whole, power = encoded(values)
    target[:rows, :] = whole
    target[rows:, :] = jnp.broadcast_to(power, (EXTRA, width)).astype(jnp.int16)


def decoded(source, lo, hi):
    rows = source.shape[0] - EXTRA
    power = source[rows:, lo:hi].astype(jnp.int32).astype(jnp.float32)[:1]
    whole = source[:rows, lo:hi].astype(jnp.int32).astype(jnp.float32)
    return whole * (jnp.exp2(power) * (1.0 / TOP))


def merge_body(kept_ref, came_ref, total_ref, coded_ref):
    total = kept_ref[...] + came_ref[...]
    total_ref[...] = total
    put_encoded(coded_ref, total)


def merge(kept, came):
    rows, width = kept.shape
    return pl.pallas_call(
        merge_body,
        out_shape=[
            jax.ShapeDtypeStruct((rows, width), jnp.float32),
            jax.ShapeDtypeStruct((rows + EXTRA, width), jnp.int16),
        ],
        cost_estimate=pl.CostEstimate(
            flops=8 * rows * width, bytes_accessed=14 * rows * width, transcendentals=0
        ),
    )(kept, came)


def turn_body(own, flag_ref, total_ref, came_ref, near_ref, leg_ref, far_ref, coded_ref):
    width = total_ref.shape[1]
    total = total_ref[...] + decoded(came_ref, 0, width)
    near_ref[...] = total[:, :own]
    put_encoded(coded_ref, total)
    far_ref[...] = coded_ref[:, own:]
    half = width - own
    first = pl.multiple_of(flag_ref[0] * half, half)
    leg_ref[...] = coded_ref[:, pl.ds(first, own)]


def turn(flag, total, came, own):
    rows, width = total.shape
    coded = lambda columns: jax.ShapeDtypeStruct((rows + EXTRA, columns), jnp.int16)
    vmem = pl.BlockSpec(memory_space=pltpu.VMEM)
    return pl.pallas_call(
        functools.partial(turn_body, own),
        grid_spec=pltpu.PrefetchScalarGridSpec(
            num_scalar_prefetch=1,
            grid=(),
            in_specs=[vmem] * 2,
            out_specs=[vmem] * 3,
            scratch_shapes=[pltpu.VMEM((rows + EXTRA, width), jnp.int16)],
        ),
        out_shape=[jax.ShapeDtypeStruct((rows, own), jnp.float32), coded(own), coded(width - own)],
        cost_estimate=pl.CostEstimate(
            flops=8 * rows * width, bytes_accessed=12 * rows * width, transcendentals=0
        ),
    )(flag, total, came)


def close_body(case_ref, own, own_came, near1, leg1, far1, near2, leg2, far2, out_ref):
    width = out_ref.shape[1]
    half = width // 2
    case = case_ref[0]

    @pl.when(case == 0)
    def _():
        out_ref[...] = own[...] + own_came[...]

    for number, near, leg in ((1, near1, leg1), (2, near2, leg2)):

        @pl.when(case == number)
        def _():
            out_ref[...] = near[...] + decoded(leg, 0, width)

    first, second = (leg1, far1), (leg2, far2)
    for number, pair in ((3, (second, first)), (4, (first, second))):

        @pl.when(case == number)
        def _():
            for i, (leg, far) in enumerate(pair):
                out_ref[:, i * half : (i + 1) * half] = decoded(leg, half, width) + decoded(far, 0, half)


def close(case, *parts):
    vmem = pl.BlockSpec(memory_space=pltpu.VMEM)
    return pl.pallas_call(
        close_body,
        grid_spec=pltpu.PrefetchScalarGridSpec(
            num_scalar_prefetch=1, grid=(), in_specs=[vmem] * len(parts), out_specs=vmem
        ),
        out_shape=jax.ShapeDtypeStruct(parts[0].shape, jnp.float32),
        name="close",
    )(case, *parts)


LINE = {t: (((t ^ 1, t), (t ^ 3, t ^ 2)), ((t ^ 2, t),)) for t in range(4)}
X, Y = 1, 2


def is_traced(value):
    return not isinstance(value, int)


def exchange_plan(chips, runs):
    flat = lambda z, c, q: (2 * z + c) * runs + q
    across = lambda bit: [(q, q ^ bit) for q in range(runs)]
    cores = [(m, m ^ 1) for m in range(2 * chips)]

    def line(target, round_):
        return [
            (flat(s, c, q), flat(t, c, q))
            for c in range(2)
            for q in range(runs)
            for s, t in LINE[target(c, q)][round_]
        ]

    def corner(target, bit):
        return [
            (flat(target(c, q), c, q), flat(target(c, q), c, q ^ bit(c)))
            for c in range(2)
            for q in range(runs)
        ]

    def around(target, bit):
        return [
            (flat(s, c, q), flat(t, c, q ^ bit(c)))
            for c in range(2)
            for q in range(runs)
            for s, t in LINE[target(c, q)][1]
        ]

    return across, cores, line, corner, around


def on_square(snapshots, block_cols, mass_blocks):
    node_count, column_count = snapshots.shape
    blk = mass_blocks.shape[1]
    blocks_here = node_count // blk
    rim = HB * blk
    half = column_count // 2
    runs = lax.axis_size("run")
    chips = lax.axis_size("mesh") // 2
    both = ("mesh", "run")
    across, cores, line, corner, around = exchange_plan(chips, runs)
    shard = lax.axis_index("mesh")
    column = lax.axis_index("run")
    core, chip = shard % 2, shard // 2
    local_cols = block_cols - (shard * blocks_here - HB)

    def over_x(v):
        return lax.ppermute(v, "run", across(X))

    def over_y(v):
        return lax.ppermute(v, "run", across(Y))

    pick = core[None].astype(jnp.int32)
    shards = 2 * chips
    low = lax.ppermute(snapshots[-rim:], "mesh", [(i, i + 1) for i in range(shards - 1)])
    high = lax.ppermute(snapshots[:rim], "mesh", [(i + 1, i) for i in range(shards - 1)])
    left = snapshots[:, :half]
    a1 = over_x(left)
    right = lax.optimization_barrier((snapshots, left))[0][:, half:]
    b2 = over_y(right)
    rims = jnp.concatenate([low, high], axis=0)
    ra = over_x(rims[:, :half])
    rb = over_y(rims[:, half:])
    a2 = over_x(right)
    b1 = over_y(left)

    top = rim + node_count

    def towards(core_a):
        return lambda c, q: q ^ jnp.where(c == core_a, X, Y) if is_traced(c) else q ^ (X, Y)[c != core_a]

    def crossing(core_a):
        return lambda c: (Y, X)[c != core_a]

    w, keep0, send0 = fused(
        local_cols, pick, mass_blocks, [low, snapshots, high],
        [(0, 0, rim, 0, 0), (1, 0, node_count, rim, 0), (2, 0, rim, top, 0)],
    )
    wx, keep1, send1 = fused(
        local_cols, pick, mass_blocks, [a1, ra, b2, rb],
        [
            (0, 0, node_count, rim, 0), (1, 0, rim, 0, 0), (1, rim, rim, top, 0),
            (2, 0, node_count, rim, half), (3, 0, rim, 0, half), (3, rim, rim, top, half),
        ],
        own=w,
    )
    keep2, send2 = fused(
        local_cols, 1 - pick, mass_blocks, [a2, b1],
        [(0, 0, node_count, 0, 0), (1, 0, node_count, 0, half)],
        own=w, extra=wx, weighs=False,
    )
    own_target = lambda c, q: q
    own = keep0 + lax.ppermute(send0, "mesh", cores)
    own = own + lax.ppermute(own, both, line(own_target, 0))
    own_came = lax.ppermute(own, both, line(own_target, 1))

    def finished(kept, sent, core_a):
        target, bit = towards(core_a), crossing(core_a)
        came = lax.ppermute(sent, "mesh", cores)
        total, coded = merge(kept, came)
        came = lax.ppermute(coded, both, line(target, 0))
        at_target = (chip == target(core, column))[None].astype(jnp.int32)
        near, leg, far = turn(at_target, total, came, column_count)
        leg = lax.ppermute(leg, both, line(target, 1) + corner(target, bit))
        far = lax.ppermute(far, both, around(target, bit))
        return near, leg, far

    stage1 = finished(keep1, send1, 0)
    stage2 = finished(keep2, send2, 1)
    near = jnp.where((chip == (column ^ X)) == (core == 0), 1, 2)
    case = jnp.where(chip == column, 0, jnp.where(chip == (column ^ (X | Y)), 3 + core, near))
    return close(case[None].astype(jnp.int32), own, own_came, *stage1, *stage2)


def on_device(snapshots, block_cols, mass_blocks):
    node_count, _ = snapshots.shape
    blk = mass_blocks.shape[1]
    blocks_here = node_count // blk
    rim = HB * blk
    shards = lax.axis_size("mesh")
    low = lax.ppermute(snapshots[-rim:], "mesh", [(i, i + 1) for i in range(shards - 1)])
    high = lax.ppermute(snapshots[:rim], "mesh", [(i + 1, i) for i in range(shards - 1)])
    local_cols = block_cols - (lax.axis_index("mesh") * blocks_here - HB)
    (weighted,) = fused(
        local_cols, jnp.zeros((1,), jnp.int32), mass_blocks, [low, snapshots, high],
        [(0, 0, rim, 0, 0), (1, 0, node_count, rim, 0), (2, 0, rim, rim + node_count, 0)],
        multiplies=False,
    )
    gathered = lax.all_gather(snapshots, "run", axis=1, tiled=True)
    return lax.psum_scatter(
        contract_nodes(gathered, weighted), "mesh", scatter_dimension=0, tiled=True
    )


def solution(mesh):
    placed = (P("mesh", "run"), P("mesh", None), P("mesh", None, None))
    square = mesh.shape["run"] == 4 and mesh.shape["mesh"] == 8

    def body(*args):
        return (on_square if square else on_device)(*args)

    return jax.shard_map(
        body, mesh=mesh, in_specs=placed, out_specs=P("mesh", "run"), check_vma=False
    )
```

```python
import functools

import jax
import jax.numpy as jnp
from jax import lax
from jax.experimental import pallas as pl
from jax.experimental.pallas import tpu as pltpu
from jax.sharding import PartitionSpec as P


HB = 2


def contract_nodes(left_cols, right_cols):
    return lax.dot_general(
        left_cols, right_cols, (((0,), (0,)), ((), ())), preferred_element_type=jnp.float32
    )


def span(start, size):
    return slice(start, start + size)


def fused_body(plan, *refs):
    refs = list(refs)
    cols_ref, pick_ref = refs.pop(0), refs.pop(0)
    mass_hbm = refs.pop(0)
    pieces = [refs.pop(0) for _ in range(plan["count"])]
    own_ref = refs.pop(0) if plan["own"] else None
    made_ref = refs.pop(0)
    keep_ref, send_ref = (refs.pop(0), refs.pop(0)) if plan["multiplies"] else (None, None)
    rows_ref = refs.pop(0)
    mass_ref = refs.pop(0)
    sems = refs.pop(0)
    blk, rim, half = plan["blk"], plan["rim"], plan["half"]

    used = iter(range(64))
    fetch = lambda source, target: pltpu.make_async_copy(source, target, sems.at[next(used)])
    rows_in = [
        fetch(pieces[p].at[span(r, n), :], rows_ref.at[span(to, n), span(lane, pieces[p].shape[1])])
        for p, r, n, to, lane in plan["places"]
    ]
    mass_in, parts = [], plan["parts"]
    size = mass_ref.shape[0] // parts
    for i in range(parts):
        part = span(i * size, size)
        mass_in.append(fetch(mass_hbm.at[part], mass_ref.at[part]))
    for copy in rows_in + mass_in:
        copy.start()
    for copy in rows_in:
        copy.wait()

    for row in range(mass_ref.shape[0]):
        if row % size == 0:
            mass_in[row // size].wait()
        picked = jnp.concatenate(
            [
                rows_ref[pl.ds(pl.multiple_of(cols_ref[row, k] * blk, blk), blk), :]
                for k in range(cols_ref.shape[1])
            ],
            axis=0,
        )
        product = jnp.dot(mass_ref[row], picked, preferred_element_type=jnp.float32)
        made_ref[row * blk : (row + 1) * blk, :] = product.astype(made_ref.dtype)

    if plan["multiplies"]:
        w_ref = own_ref if plan["own"] else made_ref
        own, nodes = w_ref.shape[1], w_ref.shape[0]
        for target, first in ((keep_ref, pick_ref[0]), (send_ref, 1 - pick_ref[0])):
            left = rows_ref[span(rim, nodes), pl.ds(pl.multiple_of(first * half, half), half)]
            target[:, :own] = contract_nodes(left, w_ref[...])
            if plan["own"]:
                right = made_ref[:, pl.ds(pl.multiple_of((1 - first) * half, half), half)]
                target[:, own:] = contract_nodes(left, right)


def in_hbm(array):
    return pltpu.with_memory_space_constraint(array, pltpu.HBM)


def parts_body(source, *refs):
    targets, sems = refs[:-1], refs[-1]
    nodes, width = source.shape
    rim = targets[-1].shape[0]
    half = width // 2
    pieces = [
        source.at[:, :half],
        source.at[:, half:],
        source.at[span(nodes - rim, rim), :],
        source.at[span(0, rim), :],
    ]
    copies = [
        pltpu.make_async_copy(piece, target, sems.at[i])
        for i, (piece, target) in enumerate(zip(pieces, targets))
    ]
    for copy in copies:
        copy.start()
    for copy in copies:
        copy.wait()


def parts_of(snapshots, rim):
    nodes, width = snapshots.shape
    shapes = [(nodes, width // 2)] * 2 + [(rim, width)] * 2
    return pl.pallas_call(
        parts_body,
        in_specs=[pl.BlockSpec(memory_space=pl.ANY)],
        out_specs=[pl.BlockSpec(memory_space=pltpu.VMEM)] * 4,
        out_shape=[pltpu.VMEM(shape, snapshots.dtype) for shape in shapes],
        scratch_shapes=[pltpu.SemaphoreType.DMA((4,))],
        compiler_params=pltpu.CompilerParams(vmem_limit_bytes=4 << 20),
        name="parts",
    )(in_hbm(snapshots))


def in_vmem(array):
    return pltpu.with_memory_space_constraint(array, pltpu.VMEM)


def fused(local_cols, pick, mass_blocks, pieces, places, own=None, multiplies=True):
    block_rows, blk, stored = mass_blocks.shape
    rim = HB * blk
    nodes = block_rows * blk
    width = max(lane + pieces[p].shape[1] for p, _, _, _, lane in places)
    half = width // 2
    row_count = max(to + n for _, _, n, to, _ in places)
    parts = 4 if block_rows % 4 == 0 else 1
    plan = dict(
        blk=blk, rim=rim, half=half, multiplies=multiplies, places=places, count=len(pieces),
        own=own is not None, parts=parts,
    )
    total = width + half if own is not None else width
    operands = [in_hbm(mass_blocks), *pieces]
    specs = [pl.BlockSpec(memory_space=pl.ANY)] * len(operands)
    if own is not None:
        operands.append(in_vmem(own))
        specs.append(pl.BlockSpec(memory_space=pltpu.VMEM))
    outs = [pltpu.VMEM((nodes, width), jnp.bfloat16)]
    flops = 8 * nodes * stored * width
    if multiplies:
        outs += [pltpu.VMEM((half, total), jnp.float32)] * 2
        flops += 4 * nodes * half * total
    return pl.pallas_call(
        functools.partial(fused_body, plan),
        grid_spec=pltpu.PrefetchScalarGridSpec(
            num_scalar_prefetch=2,
            grid=(),
            in_specs=specs,
            out_specs=[pl.BlockSpec(memory_space=pltpu.VMEM)] * len(outs),
            scratch_shapes=[
                pltpu.VMEM((row_count, width), jnp.bfloat16),
                pltpu.VMEM(mass_blocks.shape, jnp.bfloat16),
                pltpu.SemaphoreType.DMA((len(places) + parts,)),
            ],
        ),
        out_shape=outs,
        cost_estimate=pl.CostEstimate(flops=flops, bytes_accessed=8 << 20, transcendentals=0),
        compiler_params=pltpu.CompilerParams(vmem_limit_bytes=24 << 20),
    )(local_cols, pick, *operands)


def products_body(pick_ref, left_a, left_b, w_ref, x_ref, keep_ref, send_ref):
    own, half = w_ref.shape[1], x_ref.shape[1] // 2

    def multiply(target, left, lo):
        target[:, :own] = contract_nodes(left[...], w_ref[...])
        target[:, own:] = contract_nodes(left[...], x_ref[:, lo : lo + half])

    @pl.when(pick_ref[0] == 0)
    def _():
        multiply(keep_ref, left_a, half)
        multiply(send_ref, left_b, 0)

    @pl.when(pick_ref[0] != 0)
    def _():
        multiply(keep_ref, left_b, 0)
        multiply(send_ref, left_a, half)


def products(pick, left_a, left_b, w, x):
    nodes, own = w.shape
    rows, total = left_a.shape[1], own + x.shape[1] // 2
    vmem = pl.BlockSpec(memory_space=pltpu.VMEM)
    return pl.pallas_call(
        products_body,
        grid_spec=pltpu.PrefetchScalarGridSpec(
            num_scalar_prefetch=1, grid=(), in_specs=[vmem] * 4, out_specs=[vmem] * 2
        ),
        out_shape=[pltpu.VMEM((rows, total), jnp.float32)] * 2,
        cost_estimate=pl.CostEstimate(
            flops=4 * nodes * rows * total, bytes_accessed=8 << 20, transcendentals=0
        ),
        compiler_params=pltpu.CompilerParams(vmem_limit_bytes=16 << 20),
    )(pick, *(in_vmem(array) for array in (left_a, left_b, w, x)))


TOP = 32000.0
EXTRA = 16


def encoded(values):
    peak = jnp.maximum(jnp.max(jnp.abs(values), axis=0, keepdims=True), 1e-30)
    power = jnp.ceil(jnp.log2(peak))
    whole = jnp.round(values * (jnp.exp2(-power) * TOP)).astype(jnp.int32)
    return whole.astype(jnp.int16), power.astype(jnp.int32)


def put_encoded(target, values):
    rows, width = values.shape
    whole, power = encoded(values)
    target[:rows, :] = whole
    target[rows:, :] = jnp.broadcast_to(power, (EXTRA, width)).astype(jnp.int16)


def decoded(source, lo, hi):
    rows = source.shape[0] - EXTRA
    power = source[rows:, lo:hi].astype(jnp.int32).astype(jnp.float32)[:1]
    whole = source[:rows, lo:hi].astype(jnp.int32).astype(jnp.float32)
    return whole * (jnp.exp2(power) * (1.0 / TOP))


def merge_body(kept_ref, came_ref, total_ref, coded_ref):
    total = kept_ref[...] + came_ref[...]
    total_ref[...] = total
    put_encoded(coded_ref, total)


def merge(kept, came, body=merge_body):
    rows, width = kept.shape
    vmem = pl.BlockSpec(memory_space=pltpu.VMEM)
    return pl.pallas_call(
        body,
        in_specs=[vmem] * 2,
        out_specs=[vmem] * 2,
        out_shape=[
            pltpu.VMEM((rows, width), jnp.float32),
            pltpu.VMEM((rows + EXTRA, width), jnp.int16),
        ],
        cost_estimate=pl.CostEstimate(
            flops=8 * rows * width, bytes_accessed=14 * rows * width, transcendentals=0
        ),
        compiler_params=pltpu.CompilerParams(vmem_limit_bytes=16 << 20),
    )(in_vmem(kept), in_vmem(came))


def step_body(total_ref, came_ref, next_ref, coded_ref):
    total = total_ref[...] + decoded(came_ref, 0, total_ref.shape[1])
    next_ref[...] = total
    put_encoded(coded_ref, total)


def turn_body(own, flag_ref, total_ref, came_ref, near_ref, leg_ref, far_ref, coded_ref):
    width = total_ref.shape[1]
    total = total_ref[...] + decoded(came_ref, 0, width)
    near_ref[...] = total[:, :own]
    put_encoded(coded_ref, total)
    far_ref[...] = coded_ref[:, own:]
    half = width - own
    first = pl.multiple_of(flag_ref[0] * half, half)
    leg_ref[...] = coded_ref[:, pl.ds(first, own)]


def turn(flag, total, came, own):
    rows, width = total.shape
    coded = lambda columns: pltpu.VMEM((rows + EXTRA, columns), jnp.int16)
    vmem = pl.BlockSpec(memory_space=pltpu.VMEM)
    return pl.pallas_call(
        functools.partial(turn_body, own),
        grid_spec=pltpu.PrefetchScalarGridSpec(
            num_scalar_prefetch=1,
            grid=(),
            in_specs=[vmem] * 2,
            out_specs=[vmem] * 3,
            scratch_shapes=[pltpu.VMEM((rows + EXTRA, width), jnp.int16)],
        ),
        out_shape=[pltpu.VMEM((rows, own), jnp.float32), coded(own), coded(width - own)],
        cost_estimate=pl.CostEstimate(
            flops=8 * rows * width, bytes_accessed=12 * rows * width, transcendentals=0
        ),
        compiler_params=pltpu.CompilerParams(vmem_limit_bytes=16 << 20),
    )(flag, in_vmem(total), in_vmem(came))


def close_body(case_ref, own, own_came, near1, leg1, far1, near2, leg2, far2, out_ref):
    width = out_ref.shape[1]
    half = width // 2
    case = case_ref[0]

    @pl.when(case == 0)
    def _():
        out_ref[...] = own[...] + decoded(own_came, 0, width)

    for number, near, leg in ((1, near1, leg1), (2, near2, leg2)):

        @pl.when(case == number)
        def _():
            out_ref[...] = near[...] + decoded(leg, 0, width)

    first, second = (leg1, far1), (leg2, far2)
    for number, pair in ((3, (second, first)), (4, (first, second))):

        @pl.when(case == number)
        def _():
            for i, (leg, far) in enumerate(pair):
                out_ref[:, i * half : (i + 1) * half] = decoded(leg, half, width) + decoded(far, 0, half)


def close(case, *parts):
    vmem = pl.BlockSpec(memory_space=pltpu.VMEM)
    return pl.pallas_call(
        close_body,
        grid_spec=pltpu.PrefetchScalarGridSpec(
            num_scalar_prefetch=1, grid=(), in_specs=[vmem] * len(parts), out_specs=vmem
        ),
        out_shape=jax.ShapeDtypeStruct(parts[0].shape, jnp.float32),
        compiler_params=pltpu.CompilerParams(vmem_limit_bytes=16 << 20),
        name="close",
    )(case, *(in_vmem(part) for part in parts))


LINE = {t: (((t ^ 1, t), (t ^ 3, t ^ 2)), ((t ^ 2, t),)) for t in range(4)}
X, Y = 1, 2


def is_traced(value):
    return not isinstance(value, int)


def exchange_plan(chips, runs):
    flat = lambda z, c, q: (2 * z + c) * runs + q
    across = lambda bit: [(q, q ^ bit) for q in range(runs)]
    cores = [(m, m ^ 1) for m in range(2 * chips)]

    def line(target, round_):
        return [
            (flat(s, c, q), flat(t, c, q))
            for c in range(2)
            for q in range(runs)
            for s, t in LINE[target(c, q)][round_]
        ]

    def corner(target, bit):
        return [
            (flat(target(c, q), c, q), flat(target(c, q), c, q ^ bit(c)))
            for c in range(2)
            for q in range(runs)
        ]

    def around(target, bit):
        return [
            (flat(s, c, q), flat(t, c, q ^ bit(c)))
            for c in range(2)
            for q in range(runs)
            for s, t in LINE[target(c, q)][1]
        ]

    return across, cores, line, corner, around


def on_square(snapshots, block_cols, mass_blocks):
    node_count, column_count = snapshots.shape
    blk = mass_blocks.shape[1]
    blocks_here = node_count // blk
    rim = HB * blk
    half = column_count // 2
    runs = lax.axis_size("run")
    chips = lax.axis_size("mesh") // 2
    both = ("mesh", "run")
    across, cores, line, corner, around = exchange_plan(chips, runs)
    shard = lax.axis_index("mesh")
    column = lax.axis_index("run")
    core, chip = shard % 2, shard // 2
    local_cols = block_cols - (shard * blocks_here - HB)

    def over_x(v):
        return lax.ppermute(v, "run", across(X))

    def over_y(v):
        return lax.ppermute(v, "run", across(Y))

    pick = core[None].astype(jnp.int32)
    shards = 2 * chips
    left, right, last_rows, first_rows = parts_of(snapshots, rim)
    a1 = over_x(left)
    b2 = over_y(right)
    low = lax.ppermute(last_rows, "mesh", [(i, i + 1) for i in range(shards - 1)])
    high = lax.ppermute(first_rows, "mesh", [(i + 1, i) for i in range(shards - 1)])
    rims = jnp.concatenate([low, high], axis=0)
    ra = over_x(rims[:, :half])
    rb = over_y(rims[:, half:])
    a2 = over_x(right)
    b1 = over_y(left)

    top = rim + node_count

    def towards(core_a):
        return lambda c, q: q ^ jnp.where(c == core_a, X, Y) if is_traced(c) else q ^ (X, Y)[c != core_a]

    def crossing(core_a):
        return lambda c: (Y, X)[c != core_a]

    w, keep0, send0 = fused(
        local_cols, pick, mass_blocks, [low, in_hbm(snapshots), high],
        [(0, 0, rim, 0, 0), (1, 0, node_count, rim, 0), (2, 0, rim, top, 0)],
    )
    wx, keep1, send1 = fused(
        local_cols, pick, mass_blocks, [a1, ra, b2, rb],
        [
            (0, 0, node_count, rim, 0), (1, 0, rim, 0, 0), (1, rim, rim, top, 0),
            (2, 0, node_count, rim, half), (3, 0, rim, 0, half), (3, rim, rim, top, half),
        ],
        own=w,
    )
    keep2, send2 = products(1 - pick, a2, b1, w, wx)
    own_target = lambda c, q: q
    came = lax.ppermute(send0, "mesh", cores)
    own, coded = merge(keep0, came)
    came = lax.ppermute(coded, both, line(own_target, 0))
    own, coded = merge(own, came, step_body)
    own_came = lax.ppermute(coded, both, line(own_target, 1))

    def finished(kept, sent, core_a):
        target, bit = towards(core_a), crossing(core_a)
        came = lax.ppermute(sent, "mesh", cores)
        total, coded = merge(kept, came)
        came = lax.ppermute(coded, both, line(target, 0))
        at_target = (chip == target(core, column))[None].astype(jnp.int32)
        near, leg, far = turn(at_target, total, came, column_count)
        leg = lax.ppermute(leg, both, line(target, 1) + corner(target, bit))
        far = lax.ppermute(far, both, around(target, bit))
        return near, leg, far

    stage1 = finished(keep1, send1, 0)
    stage2 = finished(keep2, send2, 1)
    near = jnp.where((chip == (column ^ X)) == (core == 0), 1, 2)
    case = jnp.where(chip == column, 0, jnp.where(chip == (column ^ (X | Y)), 3 + core, near))
    return close(case[None].astype(jnp.int32), own, own_came, *stage1, *stage2)


def on_device(snapshots, block_cols, mass_blocks):
    node_count, _ = snapshots.shape
    blk = mass_blocks.shape[1]
    blocks_here = node_count // blk
    rim = HB * blk
    shards = lax.axis_size("mesh")
    low = lax.ppermute(snapshots[-rim:], "mesh", [(i, i + 1) for i in range(shards - 1)])
    high = lax.ppermute(snapshots[:rim], "mesh", [(i + 1, i) for i in range(shards - 1)])
    local_cols = block_cols - (lax.axis_index("mesh") * blocks_here - HB)
    (weighted,) = fused(
        local_cols, jnp.zeros((1,), jnp.int32), mass_blocks, [low, snapshots, high],
        [(0, 0, rim, 0, 0), (1, 0, node_count, rim, 0), (2, 0, rim, rim + node_count, 0)],
        multiplies=False,
    )
    gathered = lax.all_gather(snapshots, "run", axis=1, tiled=True)
    return lax.psum_scatter(
        contract_nodes(gathered, weighted), "mesh", scatter_dimension=0, tiled=True
    )


def solution(mesh):
    placed = (P("mesh", "run"), P("mesh", None), P("mesh", None, None))
    square = mesh.shape["run"] == 4 and mesh.shape["mesh"] == 8

    def body(*args):
        return (on_square if square else on_device)(*args)

    return jax.shard_map(
        body, mesh=mesh, in_specs=placed, out_specs=P("mesh", "run"), check_vma=False
    )
```

```python
import functools

import jax
import jax.numpy as jnp
from jax import lax
from jax.experimental import pallas as pl
from jax.experimental.pallas import tpu as pltpu
from jax.sharding import PartitionSpec as P


HB = 2


def contract_nodes(left_cols, right_cols):
    return lax.dot_general(
        left_cols, right_cols, (((0,), (0,)), ((), ())), preferred_element_type=jnp.float32
    )


def span(start, size):
    return slice(start, start + size)


def fused_body(plan, *refs):
    refs = list(refs)
    cols_ref, pick_ref = refs.pop(0), refs.pop(0)
    mass_hbm = refs.pop(0)
    pieces = [refs.pop(0) for _ in range(plan["count"])]
    made_ref = refs.pop(0)
    keep_ref, send_ref = (refs.pop(0), refs.pop(0)) if plan["multiplies"] else (None, None)
    rows_ref = refs.pop(0)
    mass_ref = refs.pop(0)
    sems = refs.pop(0)
    blk, rim, half = plan["blk"], plan["rim"], plan["half"]

    used = iter(range(64))
    fetch = lambda source, target: pltpu.make_async_copy(source, target, sems.at[next(used)])
    rows_in = [
        fetch(pieces[p].at[span(r, n), span(c, w)], rows_ref.at[span(to, n), span(lane, w)])
        for p, (r, n), (c, w), to, lane in plan["places"]
    ]
    mass_in, parts = [], plan["parts"]
    size = mass_ref.shape[0] // parts
    for i in range(parts):
        part = span(i * size, size)
        mass_in.append(fetch(mass_hbm.at[part], mass_ref.at[part]))
    for copy in rows_in + mass_in:
        copy.start()
    for copy in rows_in:
        copy.wait()

    for row in range(mass_ref.shape[0]):
        if row % size == 0:
            mass_in[row // size].wait()
        picked = jnp.concatenate(
            [
                rows_ref[pl.ds(pl.multiple_of(cols_ref[row, k] * blk, blk), blk), :]
                for k in range(cols_ref.shape[1])
            ],
            axis=0,
        )
        product = jnp.dot(mass_ref[row], picked, preferred_element_type=jnp.float32)
        made_ref[row * blk : (row + 1) * blk, :] = product.astype(made_ref.dtype)

    if plan["multiplies"]:
        own, nodes = made_ref.shape[1], made_ref.shape[0]
        for target, first in ((keep_ref, pick_ref[0]), (send_ref, 1 - pick_ref[0])):
            left = rows_ref[span(rim, nodes), pl.ds(pl.multiple_of(first * half, half), half)]
            target[:, :own] = contract_nodes(left, made_ref[...])


def in_hbm(array):
    return pltpu.with_memory_space_constraint(array, pltpu.HBM)


def parts_body(cuts, source, *refs):
    targets, sems = refs[:-1], refs[-1]
    copies = []
    for pieces, target in zip(cuts, targets):
        done = 0
        for (r, n), (c, w) in pieces:
            copies.append(
                pltpu.make_async_copy(
                    source.at[span(r, n), span(c, w)],
                    target.at[span(done, n), :],
                    sems.at[len(copies)],
                )
            )
            done += n
    for copy in copies:
        copy.start()
    for copy in copies:
        copy.wait()


def parts_of(array, *cuts):
    shapes = [(sum(n for (_, n), _ in pieces), pieces[0][1][1]) for pieces in cuts]
    return pl.pallas_call(
        functools.partial(parts_body, cuts),
        in_specs=[pl.BlockSpec(memory_space=pl.ANY)],
        out_specs=[pl.BlockSpec(memory_space=pltpu.VMEM)] * len(cuts),
        out_shape=[pltpu.VMEM(shape, array.dtype) for shape in shapes],
        scratch_shapes=[pltpu.SemaphoreType.DMA((sum(len(pieces) for pieces in cuts),))],
        compiler_params=pltpu.CompilerParams(vmem_limit_bytes=4 << 20),
    )(in_hbm(array))


def rims_body(*refs):
    edges, (last_ref, first_ref) = refs[:-2], refs[-2:]
    rim = last_ref.shape[0]
    lane = 0
    for edge in edges:
        place = span(lane, edge.shape[1])
        first_ref[:, place] = edge[:rim, :]
        last_ref[:, place] = edge[rim:, :]
        lane += edge.shape[1]


def rims_of(*edges):
    vmem = pl.BlockSpec(memory_space=pltpu.VMEM)
    shape = (edges[0].shape[0] // 2, sum(edge.shape[1] for edge in edges))
    return pl.pallas_call(
        rims_body,
        in_specs=[vmem] * len(edges),
        out_specs=[vmem] * 2,
        out_shape=[pltpu.VMEM(shape, edges[0].dtype)] * 2,
        compiler_params=pltpu.CompilerParams(vmem_limit_bytes=4 << 20),
        name="rims",
    )(*(in_vmem(edge) for edge in edges))


def in_vmem(array):
    return pltpu.with_memory_space_constraint(array, pltpu.VMEM)


def fused(local_cols, pick, mass_blocks, pieces, places, multiplies=True, hands_out=False):
    block_rows, blk, stored = mass_blocks.shape
    rim = HB * blk
    nodes = block_rows * blk
    width = max(lane + w for _, _, (_, w), _, lane in places)
    half = width // 2
    row_count = max(to + n for _, (_, n), _, to, _ in places)
    parts = 4 if block_rows % 4 == 0 else 1
    plan = dict(
        blk=blk, rim=rim, half=half, multiplies=multiplies, places=places, count=len(pieces),
        parts=parts,
    )
    operands = [in_hbm(mass_blocks), *pieces]
    specs = [pl.BlockSpec(memory_space=pl.ANY)] * len(operands)
    outs = [pltpu.VMEM((nodes, width), jnp.bfloat16)]
    flops = 8 * nodes * stored * width
    if multiplies:
        outs += [pltpu.VMEM((half, width), jnp.float32)] * 2
        flops += 4 * nodes * half * width
    rows = [pltpu.VMEM((row_count, width), jnp.bfloat16)]
    outs, scratch = (outs + rows, []) if hands_out else (outs, rows)
    return pl.pallas_call(
        functools.partial(fused_body, plan),
        grid_spec=pltpu.PrefetchScalarGridSpec(
            num_scalar_prefetch=2,
            grid=(),
            in_specs=specs,
            out_specs=[pl.BlockSpec(memory_space=pltpu.VMEM)] * len(outs),
            scratch_shapes=[
                *scratch,
                pltpu.VMEM(mass_blocks.shape, jnp.bfloat16),
                pltpu.SemaphoreType.DMA((len(places) + parts,)),
            ],
        ),
        out_shape=outs,
        cost_estimate=pl.CostEstimate(flops=flops, bytes_accessed=8 << 20, transcendentals=0),
        compiler_params=pltpu.CompilerParams(vmem_limit_bytes=24 << 20),
    )(local_cols, pick, *operands)


def products_body(pick_ref, left_a, left_b, w_ref, x_ref, keep_ref, send_ref):
    own, half = w_ref.shape[1], x_ref.shape[1] // 2

    def multiply(target, left, lo):
        target[:, :own] = contract_nodes(left[...], w_ref[...])
        target[:, own:] = contract_nodes(left[...], x_ref[:, lo : lo + half])

    @pl.when(pick_ref[0] == 0)
    def _():
        multiply(keep_ref, left_a, half)
        multiply(send_ref, left_b, 0)

    @pl.when(pick_ref[0] != 0)
    def _():
        multiply(keep_ref, left_b, 0)
        multiply(send_ref, left_a, half)


def products_of_rows_body(rim, pick_ref, rows_ref, w_ref, x_ref, keep_ref, send_ref):
    own, nodes, half = w_ref.shape[1], w_ref.shape[0], x_ref.shape[1] // 2
    for target, first in ((keep_ref, pick_ref[0]), (send_ref, 1 - pick_ref[0])):
        left = rows_ref[span(rim, nodes), pl.ds(pl.multiple_of(first * half, half), half)]
        target[:, :own] = contract_nodes(left, w_ref[...])
        right = x_ref[:, pl.ds(pl.multiple_of((1 - first) * half, half), half)]
        target[:, own:] = contract_nodes(left, right)


def products_of_rows(pick, rows, rim, w, x):
    nodes, own = w.shape
    half = x.shape[1] // 2
    vmem = pl.BlockSpec(memory_space=pltpu.VMEM)
    return pl.pallas_call(
        functools.partial(products_of_rows_body, rim),
        grid_spec=pltpu.PrefetchScalarGridSpec(
            num_scalar_prefetch=1, grid=(), in_specs=[vmem] * 3, out_specs=[vmem] * 2
        ),
        out_shape=[pltpu.VMEM((half, own + half), jnp.float32)] * 2,
        cost_estimate=pl.CostEstimate(
            flops=4 * nodes * half * (own + half), bytes_accessed=8 << 20, transcendentals=0
        ),
        compiler_params=pltpu.CompilerParams(vmem_limit_bytes=16 << 20),
    )(pick, *(in_vmem(array) for array in (rows, w, x)))


def products(pick, left_a, left_b, w, x):
    nodes, own = w.shape
    rows, total = left_a.shape[1], own + x.shape[1] // 2
    vmem = pl.BlockSpec(memory_space=pltpu.VMEM)
    return pl.pallas_call(
        products_body,
        grid_spec=pltpu.PrefetchScalarGridSpec(
            num_scalar_prefetch=1, grid=(), in_specs=[vmem] * 4, out_specs=[vmem] * 2
        ),
        out_shape=[pltpu.VMEM((rows, total), jnp.float32)] * 2,
        cost_estimate=pl.CostEstimate(
            flops=4 * nodes * rows * total, bytes_accessed=8 << 20, transcendentals=0
        ),
        compiler_params=pltpu.CompilerParams(vmem_limit_bytes=16 << 20),
    )(pick, *(in_vmem(array) for array in (left_a, left_b, w, x)))


TOP = 32000.0
EXTRA = 16


def encoded(values):
    peak = jnp.maximum(jnp.max(jnp.abs(values), axis=0, keepdims=True), 1e-30)
    power = jnp.ceil(jnp.log2(peak))
    whole = jnp.round(values * (jnp.exp2(-power) * TOP)).astype(jnp.int32)
    return whole.astype(jnp.int16), power.astype(jnp.int32)


def put_encoded(target, values):
    rows, width = values.shape
    whole, power = encoded(values)
    target[:rows, :] = whole
    target[rows:, :] = jnp.broadcast_to(power, (EXTRA, width)).astype(jnp.int16)


def decoded(source, lo, hi):
    rows = source.shape[0] - EXTRA
    power = source[rows:, lo:hi].astype(jnp.int32).astype(jnp.float32)[:1]
    whole = source[:rows, lo:hi].astype(jnp.int32).astype(jnp.float32)
    return whole * (jnp.exp2(power) * (1.0 / TOP))


def merge_body(kept_ref, came_ref, total_ref, coded_ref):
    total = kept_ref[...] + came_ref[...]
    total_ref[...] = total
    put_encoded(coded_ref, total)


def merge(kept, came, body=merge_body):
    rows, width = kept.shape
    vmem = pl.BlockSpec(memory_space=pltpu.VMEM)
    return pl.pallas_call(
        body,
        in_specs=[vmem] * 2,
        out_specs=[vmem] * 2,
        out_shape=[
            pltpu.VMEM((rows, width), jnp.float32),
            pltpu.VMEM((rows + EXTRA, width), jnp.int16),
        ],
        cost_estimate=pl.CostEstimate(
            flops=8 * rows * width, bytes_accessed=14 * rows * width, transcendentals=0
        ),
        compiler_params=pltpu.CompilerParams(vmem_limit_bytes=16 << 20),
    )(in_vmem(kept), in_vmem(came))


def step_body(total_ref, came_ref, next_ref, coded_ref):
    total = total_ref[...] + decoded(came_ref, 0, total_ref.shape[1])
    next_ref[...] = total
    put_encoded(coded_ref, total)


def turn_body(own, flag_ref, total_ref, came_ref, near_ref, leg_ref, far_ref, coded_ref):
    width = total_ref.shape[1]
    total = total_ref[...] + decoded(came_ref, 0, width)
    near_ref[...] = total[:, :own]
    put_encoded(coded_ref, total)
    far_ref[...] = coded_ref[:, own:]
    half = width - own
    first = pl.multiple_of(flag_ref[0] * half, half)
    leg_ref[...] = coded_ref[:, pl.ds(first, own)]


def turn(flag, total, came, own):
    rows, width = total.shape
    coded = lambda columns: pltpu.VMEM((rows + EXTRA, columns), jnp.int16)
    vmem = pl.BlockSpec(memory_space=pltpu.VMEM)
    return pl.pallas_call(
        functools.partial(turn_body, own),
        grid_spec=pltpu.PrefetchScalarGridSpec(
            num_scalar_prefetch=1,
            grid=(),
            in_specs=[vmem] * 2,
            out_specs=[vmem] * 3,
            scratch_shapes=[pltpu.VMEM((rows + EXTRA, width), jnp.int16)],
        ),
        out_shape=[pltpu.VMEM((rows, own), jnp.float32), coded(own), coded(width - own)],
        cost_estimate=pl.CostEstimate(
            flops=8 * rows * width, bytes_accessed=12 * rows * width, transcendentals=0
        ),
        compiler_params=pltpu.CompilerParams(vmem_limit_bytes=16 << 20),
    )(flag, in_vmem(total), in_vmem(came))


def close_body(case_ref, own, own_came, near1, leg1, far1, near2, leg2, far2, out_ref):
    width = out_ref.shape[1]
    half = width // 2
    case = case_ref[0]

    @pl.when(case == 0)
    def _():
        out_ref[...] = own[...] + decoded(own_came, 0, width)

    for number, near, leg in ((1, near1, leg1), (2, near2, leg2)):

        @pl.when(case == number)
        def _():
            out_ref[...] = near[...] + decoded(leg, 0, width)

    first, second = (leg1, far1), (leg2, far2)
    for number, pair in ((3, (second, first)), (4, (first, second))):

        @pl.when(case == number)
        def _():
            for i, (leg, far) in enumerate(pair):
                out_ref[:, i * half : (i + 1) * half] = decoded(leg, half, width) + decoded(far, 0, half)


def close(case, *parts):
    vmem = pl.BlockSpec(memory_space=pltpu.VMEM)
    return pl.pallas_call(
        close_body,
        grid_spec=pltpu.PrefetchScalarGridSpec(
            num_scalar_prefetch=1, grid=(), in_specs=[vmem] * len(parts), out_specs=vmem
        ),
        out_shape=jax.ShapeDtypeStruct(parts[0].shape, jnp.float32),
        compiler_params=pltpu.CompilerParams(vmem_limit_bytes=16 << 20),
        name="close",
    )(case, *(in_vmem(part) for part in parts))


LINE = {t: (((t ^ 1, t), (t ^ 3, t ^ 2)), ((t ^ 2, t),)) for t in range(4)}
X, Y = 1, 2


def is_traced(value):
    return not isinstance(value, int)


def exchange_plan(chips, runs):
    flat = lambda z, c, q: (2 * z + c) * runs + q
    across = lambda bit: [(q, q ^ bit) for q in range(runs)]
    cores = [(m, m ^ 1) for m in range(2 * chips)]

    def line(target, round_):
        return [
            (flat(s, c, q), flat(t, c, q))
            for c in range(2)
            for q in range(runs)
            for s, t in LINE[target(c, q)][round_]
        ]

    def corner(target, bit):
        return [
            (flat(target(c, q), c, q), flat(target(c, q), c, q ^ bit(c)))
            for c in range(2)
            for q in range(runs)
        ]

    def around(target, bit):
        return [
            (flat(s, c, q), flat(t, c, q ^ bit(c)))
            for c in range(2)
            for q in range(runs)
            for s, t in LINE[target(c, q)][1]
        ]

    return across, cores, line, corner, around


def on_square(snapshots, block_cols, mass_blocks):
    node_count, column_count = snapshots.shape
    blk = mass_blocks.shape[1]
    blocks_here = node_count // blk
    rim = HB * blk
    half = column_count // 2
    runs = lax.axis_size("run")
    chips = lax.axis_size("mesh") // 2
    both = ("mesh", "run")
    across, cores, line, corner, around = exchange_plan(chips, runs)
    shard = lax.axis_index("mesh")
    column = lax.axis_index("run")
    core, chip = shard % 2, shard // 2
    local_cols = block_cols - (shard * blocks_here - HB)

    def over_x(v):
        return lax.ppermute(v, "run", across(X))

    def over_y(v):
        return lax.ppermute(v, "run", across(Y))

    pick = core[None].astype(jnp.int32)
    shards = 2 * chips
    west, east = (0, half), (half, half)
    middle = (rim, node_count - 2 * rim)
    ends = (0, rim), (node_count - rim, rim)
    left_edge, right_edge = parts_of(
        snapshots, *(tuple((end, side) for end in ends) for side in (west, east))
    )
    a_edge = over_x(left_edge)
    b_edge = over_y(right_edge)
    left_middle, right_middle = parts_of(snapshots, ((middle, west),), ((middle, east),))
    a1 = over_x(left_middle)
    b2 = over_y(right_middle)
    last_rows, first_rows = rims_of(left_edge, right_edge, a_edge, b_edge)
    low = lax.ppermute(last_rows, "mesh", [(i, i + 1) for i in range(shards - 1)])
    high = lax.ppermute(first_rows, "mesh", [(i + 1, i) for i in range(shards - 1)])
    left, right = parts_of(snapshots, (((0, node_count), west),), (((0, node_count), east),))
    a2 = over_x(right)
    b1 = over_y(left)

    top = rim + node_count
    all_rows, every = (0, rim), (0, column_count)

    def towards(core_a):
        return lambda c, q: q ^ jnp.where(c == core_a, X, Y) if is_traced(c) else q ^ (X, Y)[c != core_a]

    def crossing(core_a):
        return lambda c: (Y, X)[c != core_a]

    w, keep0, send0 = fused(
        local_cols, pick, mass_blocks, [low, in_hbm(snapshots), high],
        [
            (0, all_rows, every, 0, 0), (1, (0, node_count), every, rim, 0),
            (2, all_rows, every, top, 0),
        ],
    )
    beyond = (column_count, column_count)
    near_rows = [
        (piece, rows, (0, half), rim + to, lane)
        for edge, inner, lane in ((2, 3, 0), (4, 5, half))
        for piece, rows, to in (
            (edge, (0, rim), 0),
            (inner, (0, node_count - 2 * rim), rim),
            (edge, (rim, rim), node_count - rim),
        )
    ]
    wx, rows = fused(
        local_cols, pick, mass_blocks, [low, high, a_edge, a1, b_edge, b2],
        [(0, all_rows, beyond, 0, 0), (1, all_rows, beyond, top, 0), *near_rows],
        multiplies=False, hands_out=True,
    )
    keep1, send1 = products_of_rows(pick, rows, rim, w, wx)
    keep2, send2 = products(1 - pick, a2, b1, w, wx)
    own_target = lambda c, q: q
    came = lax.ppermute(send0, "mesh", cores)
    own, coded = merge(keep0, came)
    came = lax.ppermute(coded, both, line(own_target, 0))
    own, coded = merge(own, came, step_body)
    own_came = lax.ppermute(coded, both, line(own_target, 1))

    def finished(kept, sent, core_a):
        target, bit = towards(core_a), crossing(core_a)
        came = lax.ppermute(sent, "mesh", cores)
        total, coded = merge(kept, came)
        came = lax.ppermute(coded, both, line(target, 0))
        at_target = (chip == target(core, column))[None].astype(jnp.int32)
        near, leg, far = turn(at_target, total, came, column_count)
        leg = lax.ppermute(leg, both, line(target, 1) + corner(target, bit))
        far = lax.ppermute(far, both, around(target, bit))
        return near, leg, far

    stage1 = finished(keep1, send1, 0)
    stage2 = finished(keep2, send2, 1)
    near = jnp.where((chip == (column ^ X)) == (core == 0), 1, 2)
    case = jnp.where(chip == column, 0, jnp.where(chip == (column ^ (X | Y)), 3 + core, near))
    return close(case[None].astype(jnp.int32), own, own_came, *stage1, *stage2)


def on_device(snapshots, block_cols, mass_blocks):
    node_count, column_count = snapshots.shape
    blk = mass_blocks.shape[1]
    blocks_here = node_count // blk
    rim = HB * blk
    shards = lax.axis_size("mesh")
    low = lax.ppermute(snapshots[-rim:], "mesh", [(i, i + 1) for i in range(shards - 1)])
    high = lax.ppermute(snapshots[:rim], "mesh", [(i + 1, i) for i in range(shards - 1)])
    local_cols = block_cols - (lax.axis_index("mesh") * blocks_here - HB)
    (weighted,) = fused(
        local_cols, jnp.zeros((1,), jnp.int32), mass_blocks, [low, snapshots, high],
        [
            (0, (0, rim), (0, column_count), 0, 0),
            (1, (0, node_count), (0, column_count), rim, 0),
            (2, (0, rim), (0, column_count), rim + node_count, 0),
        ],
        multiplies=False,
    )
    gathered = lax.all_gather(snapshots, "run", axis=1, tiled=True)
    return lax.psum_scatter(
        contract_nodes(gathered, weighted), "mesh", scatter_dimension=0, tiled=True
    )


def solution(mesh):
    placed = (P("mesh", "run"), P("mesh", None), P("mesh", None, None))
    square = mesh.shape["run"] == 4 and mesh.shape["mesh"] == 8

    def body(*args):
        return (on_square if square else on_device)(*args)

    return jax.shard_map(
        body, mesh=mesh, in_specs=placed, out_specs=P("mesh", "run"), check_vma=False
    )
```

```python
import functools

import jax
import jax.numpy as jnp
from jax import lax
from jax.experimental import pallas as pl
from jax.experimental.pallas import tpu as pltpu
from jax.sharding import PartitionSpec as P


HB = 2


def contract_nodes(left_cols, right_cols):
    return lax.dot_general(
        left_cols, right_cols, (((0,), (0,)), ((), ())), preferred_element_type=jnp.float32
    )


def span(start, size):
    return slice(start, start + size)


def fused_body(plan, *refs):
    refs = list(refs)
    cols_ref, pick_ref = refs.pop(0), refs.pop(0)
    mass_hbm = refs.pop(0)
    pieces = [refs.pop(0) for _ in range(plan["count"])]
    made_ref = refs.pop(0)
    keep_ref, send_ref = (refs.pop(0), refs.pop(0)) if plan["multiplies"] else (None, None)
    side_ref = refs.pop(0) if plan["hands_out"] else None
    rows_ref = refs.pop(0)
    mass_ref = refs.pop(0)
    sems = refs.pop(0)
    blk, rim, half = plan["blk"], plan["rim"], plan["half"]

    used = iter(range(64))
    fetch = lambda source, target: pltpu.make_async_copy(source, target, sems.at[next(used)])
    rows_in = [
        fetch(pieces[p].at[span(r, n), span(c, w)], rows_ref.at[span(to, n), span(lane, w)])
        for p, (r, n), (c, w), to, lane in plan["places"]
    ]
    mass_in, parts = [], plan["parts"]
    size = mass_ref.shape[0] // parts
    for i in range(parts):
        part = span(i * size, size)
        mass_in.append(fetch(mass_hbm.at[part], mass_ref.at[part]))
    for copy in rows_in + mass_in:
        copy.start()
    for copy in rows_in:
        copy.wait()

    for row in range(mass_ref.shape[0]):
        if row % size == 0:
            mass_in[row // size].wait()
        picked = jnp.concatenate(
            [
                rows_ref[pl.ds(pl.multiple_of(cols_ref[row, k] * blk, blk), blk), :]
                for k in range(cols_ref.shape[1])
            ],
            axis=0,
        )
        product = jnp.dot(mass_ref[row], picked, preferred_element_type=jnp.float32)
        made_ref[row * blk : (row + 1) * blk, :] = product.astype(made_ref.dtype)

    if plan["hands_out"]:
        side_ref[...] = made_ref[:, pl.ds(pl.multiple_of((1 - pick_ref[0]) * half, half), half)]
    if plan["multiplies"]:
        own, nodes = made_ref.shape[1], made_ref.shape[0]
        for target, first in ((keep_ref, pick_ref[0]), (send_ref, 1 - pick_ref[0])):
            left = rows_ref[span(rim, nodes), pl.ds(pl.multiple_of(first * half, half), half)]
            target[:, :own] = contract_nodes(left, made_ref[...])


def in_hbm(array):
    return pltpu.with_memory_space_constraint(array, pltpu.HBM)


def parts_body(cuts, source, *refs):
    targets, sems = refs[:-1], refs[-1]
    copies = []
    for pieces, target in zip(cuts, targets):
        done = 0
        for (r, n), (c, w) in pieces:
            copies.append(
                pltpu.make_async_copy(
                    source.at[span(r, n), span(c, w)],
                    target.at[span(done, n), :],
                    sems.at[len(copies)],
                )
            )
            done += n
    for copy in copies:
        copy.start()
    for copy in copies:
        copy.wait()


def parts_of(array, *cuts):
    shapes = [(sum(n for (_, n), _ in pieces), pieces[0][1][1]) for pieces in cuts]
    return pl.pallas_call(
        functools.partial(parts_body, cuts),
        in_specs=[pl.BlockSpec(memory_space=pl.ANY)],
        out_specs=[pl.BlockSpec(memory_space=pltpu.VMEM)] * len(cuts),
        out_shape=[pltpu.VMEM(shape, array.dtype) for shape in shapes],
        scratch_shapes=[pltpu.SemaphoreType.DMA((sum(len(pieces) for pieces in cuts),))],
        compiler_params=pltpu.CompilerParams(vmem_limit_bytes=4 << 20),
    )(in_hbm(array))


def sides_body(pick_ref, source, first_ref, second_ref, sems):
    half = first_ref.shape[1]
    copies = []
    for target, side in ((first_ref, pick_ref[0]), (second_ref, 1 - pick_ref[0])):
        piece = source.at[:, pl.ds(pl.multiple_of(side * half, half), half)]
        copies.append(pltpu.make_async_copy(piece, target, sems.at[len(copies)]))
    for copy in copies:
        copy.start()
    for copy in copies:
        copy.wait()


def sides_of(pick, array):
    nodes, width = array.shape
    return pl.pallas_call(
        sides_body,
        grid_spec=pltpu.PrefetchScalarGridSpec(
            num_scalar_prefetch=1,
            grid=(),
            in_specs=[pl.BlockSpec(memory_space=pl.ANY)],
            out_specs=[pl.BlockSpec(memory_space=pltpu.VMEM)] * 2,
            scratch_shapes=[pltpu.SemaphoreType.DMA((2,))],
        ),
        out_shape=[pltpu.VMEM((nodes, width // 2), array.dtype)] * 2,
        compiler_params=pltpu.CompilerParams(vmem_limit_bytes=4 << 20),
    )(pick, in_hbm(array))


def rims_body(*refs):
    edges, (last_ref, first_ref) = refs[:-2], refs[-2:]
    rim = last_ref.shape[0]
    lane = 0
    for edge in edges:
        place = span(lane, edge.shape[1])
        first_ref[:, place] = edge[:rim, :]
        last_ref[:, place] = edge[rim:, :]
        lane += edge.shape[1]


def rims_of(*edges):
    vmem = pl.BlockSpec(memory_space=pltpu.VMEM)
    shape = (edges[0].shape[0] // 2, sum(edge.shape[1] for edge in edges))
    return pl.pallas_call(
        rims_body,
        in_specs=[vmem] * len(edges),
        out_specs=[vmem] * 2,
        out_shape=[pltpu.VMEM(shape, edges[0].dtype)] * 2,
        compiler_params=pltpu.CompilerParams(vmem_limit_bytes=4 << 20),
        name="rims",
    )(*(in_vmem(edge) for edge in edges))


def in_vmem(array):
    return pltpu.with_memory_space_constraint(array, pltpu.VMEM)


def fused(local_cols, pick, mass_blocks, pieces, places, multiplies=True, hands_out=False):
    block_rows, blk, stored = mass_blocks.shape
    rim = HB * blk
    nodes = block_rows * blk
    width = max(lane + w for _, _, (_, w), _, lane in places)
    half = width // 2
    row_count = max(to + n for _, (_, n), _, to, _ in places)
    parts = 4 if block_rows % 4 == 0 else 1
    plan = dict(
        blk=blk, rim=rim, half=half, multiplies=multiplies, places=places, count=len(pieces),
        parts=parts, hands_out=hands_out,
    )
    operands = [in_hbm(mass_blocks), *pieces]
    specs = [pl.BlockSpec(memory_space=pl.ANY)] * len(operands)
    outs = [pltpu.VMEM((nodes, width), jnp.bfloat16)]
    flops = 8 * nodes * stored * width
    if multiplies:
        outs += [pltpu.VMEM((half, width), jnp.float32)] * 2
        flops += 4 * nodes * half * width
    rows = [pltpu.VMEM((row_count, width), jnp.bfloat16)]
    side = [pltpu.VMEM((nodes, half), jnp.bfloat16)]
    outs, scratch = (outs + side + rows, []) if hands_out else (outs, rows)
    return pl.pallas_call(
        functools.partial(fused_body, plan),
        grid_spec=pltpu.PrefetchScalarGridSpec(
            num_scalar_prefetch=2,
            grid=(),
            in_specs=specs,
            out_specs=[pl.BlockSpec(memory_space=pltpu.VMEM)] * len(outs),
            scratch_shapes=[
                *scratch,
                pltpu.VMEM(mass_blocks.shape, jnp.bfloat16),
                pltpu.SemaphoreType.DMA((len(places) + parts,)),
            ],
        ),
        out_shape=outs,
        cost_estimate=pl.CostEstimate(flops=flops, bytes_accessed=8 << 20, transcendentals=0),
        compiler_params=pltpu.CompilerParams(vmem_limit_bytes=24 << 20),
    )(local_cols, pick, *operands)


def products_of_rows_body(rim, pick_ref, rows_ref, w_ref, x_ref, keep_ref, send_ref):
    own, nodes, half = w_ref.shape[1], w_ref.shape[0], x_ref.shape[1] // 2
    for target, first in ((keep_ref, pick_ref[0]), (send_ref, 1 - pick_ref[0])):
        left = rows_ref[span(rim, nodes), pl.ds(pl.multiple_of(first * half, half), half)]
        target[:, :own] = contract_nodes(left, w_ref[...])
        right = x_ref[:, pl.ds(pl.multiple_of((1 - first) * half, half), half)]
        target[:, own:] = contract_nodes(left, right)


def products_of_rows(pick, rows, rim, w, x):
    nodes, own = w.shape
    half = x.shape[1] // 2
    vmem = pl.BlockSpec(memory_space=pltpu.VMEM)
    return pl.pallas_call(
        functools.partial(products_of_rows_body, rim),
        grid_spec=pltpu.PrefetchScalarGridSpec(
            num_scalar_prefetch=1, grid=(), in_specs=[vmem] * 3, out_specs=[vmem] * 2
        ),
        out_shape=[pltpu.VMEM((half, own + half), jnp.float32)] * 2,
        cost_estimate=pl.CostEstimate(
            flops=4 * nodes * half * (own + half), bytes_accessed=8 << 20, transcendentals=0
        ),
        compiler_params=pltpu.CompilerParams(vmem_limit_bytes=16 << 20),
    )(pick, *(in_vmem(array) for array in (rows, w, x)))


TOP = 32000.0
EXTRA = 16


def encoded(values):
    peak = jnp.maximum(jnp.max(jnp.abs(values), axis=0, keepdims=True), 1e-30)
    power = jnp.ceil(jnp.log2(peak))
    whole = jnp.round(values * (jnp.exp2(-power) * TOP)).astype(jnp.int32)
    return whole.astype(jnp.int16), power.astype(jnp.int32)


def put_encoded(target, values):
    rows, width = values.shape
    whole, power = encoded(values)
    target[:rows, :] = whole
    target[rows:, :] = jnp.broadcast_to(power, (EXTRA, width)).astype(jnp.int16)


def decoded(source, lo, hi):
    rows = source.shape[0] - EXTRA
    power = source[rows:, lo:hi].astype(jnp.int32).astype(jnp.float32)[:1]
    whole = source[:rows, lo:hi].astype(jnp.int32).astype(jnp.float32)
    return whole * (jnp.exp2(power) * (1.0 / TOP))


def merge_body(kept_ref, came_ref, total_ref, coded_ref):
    total = kept_ref[...] + came_ref[...]
    total_ref[...] = total
    put_encoded(coded_ref, total)


def merge(kept, came, body=merge_body):
    rows, width = kept.shape
    vmem = pl.BlockSpec(memory_space=pltpu.VMEM)
    return pl.pallas_call(
        body,
        in_specs=[vmem] * 2,
        out_specs=[vmem] * 2,
        out_shape=[
            pltpu.VMEM((rows, width), jnp.float32),
            pltpu.VMEM((rows + EXTRA, width), jnp.int16),
        ],
        cost_estimate=pl.CostEstimate(
            flops=8 * rows * width, bytes_accessed=14 * rows * width, transcendentals=0
        ),
        compiler_params=pltpu.CompilerParams(vmem_limit_bytes=16 << 20),
    )(in_vmem(kept), in_vmem(came))


def step_body(total_ref, came_ref, next_ref, coded_ref):
    total = total_ref[...] + decoded(came_ref, 0, total_ref.shape[1])
    next_ref[...] = total
    put_encoded(coded_ref, total)


def chip_body(pick_ref, left, left_too, w, w_too, x, x_too, total_ref, coded_ref):
    own, half = w.shape[1], x_too.shape[1]
    side = x[:, pl.ds(pl.multiple_of(pick_ref[0] * half, half), half)]
    near = contract_nodes(left[...], w[...]) + contract_nodes(left_too[...], w_too[...])
    total_ref[:, :own] = near
    total_ref[:, own:] = contract_nodes(left[...], side) + contract_nodes(left_too[...], x_too[...])
    put_encoded(coded_ref, total_ref[...])


def chip_products(pick, *operands):
    left, _, w, _, _, x_too = operands
    nodes, rows = left.shape
    total = w.shape[1] + x_too.shape[1]
    vmem = pl.BlockSpec(memory_space=pltpu.VMEM)
    return pl.pallas_call(
        chip_body,
        grid_spec=pltpu.PrefetchScalarGridSpec(
            num_scalar_prefetch=1, grid=(), in_specs=[vmem] * 6, out_specs=[vmem] * 2
        ),
        out_shape=[
            pltpu.VMEM((rows, total), jnp.float32),
            pltpu.VMEM((rows + EXTRA, total), jnp.int16),
        ],
        cost_estimate=pl.CostEstimate(
            flops=4 * nodes * rows * total, bytes_accessed=8 << 20, transcendentals=0
        ),
        compiler_params=pltpu.CompilerParams(vmem_limit_bytes=16 << 20),
    )(pick, *(in_vmem(operand) for operand in operands))


def turn_body(own, flag_ref, total_ref, came_ref, near_ref, leg_ref, far_ref, coded_ref):
    width = total_ref.shape[1]
    total = total_ref[...] + decoded(came_ref, 0, width)
    near_ref[...] = total[:, :own]
    put_encoded(coded_ref, total)
    far_ref[...] = coded_ref[:, own:]
    half = width - own
    first = pl.multiple_of(flag_ref[0] * half, half)
    leg_ref[...] = coded_ref[:, pl.ds(first, own)]


def turn(flag, total, came, own):
    rows, width = total.shape
    coded = lambda columns: pltpu.VMEM((rows + EXTRA, columns), jnp.int16)
    vmem = pl.BlockSpec(memory_space=pltpu.VMEM)
    return pl.pallas_call(
        functools.partial(turn_body, own),
        grid_spec=pltpu.PrefetchScalarGridSpec(
            num_scalar_prefetch=1,
            grid=(),
            in_specs=[vmem] * 2,
            out_specs=[vmem] * 3,
            scratch_shapes=[pltpu.VMEM((rows + EXTRA, width), jnp.int16)],
        ),
        out_shape=[pltpu.VMEM((rows, own), jnp.float32), coded(own), coded(width - own)],
        cost_estimate=pl.CostEstimate(
            flops=8 * rows * width, bytes_accessed=12 * rows * width, transcendentals=0
        ),
        compiler_params=pltpu.CompilerParams(vmem_limit_bytes=16 << 20),
    )(flag, in_vmem(total), in_vmem(came))


def close_body(case_ref, own, own_came, near1, leg1, far1, near2, leg2, far2, out_ref):
    width = out_ref.shape[1]
    half = width // 2
    case = case_ref[0]

    @pl.when(case == 0)
    def _():
        out_ref[...] = own[...] + decoded(own_came, 0, width)

    for number, near, leg in ((1, near1, leg1), (2, near2, leg2)):

        @pl.when(case == number)
        def _():
            out_ref[...] = near[...] + decoded(leg, 0, width)

    first, second = (leg1, far1), (leg2, far2)
    for number, pair in ((3, (second, first)), (4, (first, second))):

        @pl.when(case == number)
        def _():
            for i, (leg, far) in enumerate(pair):
                out_ref[:, i * half : (i + 1) * half] = decoded(leg, half, width) + decoded(far, 0, half)


def close(case, *parts):
    vmem = pl.BlockSpec(memory_space=pltpu.VMEM)
    return pl.pallas_call(
        close_body,
        grid_spec=pltpu.PrefetchScalarGridSpec(
            num_scalar_prefetch=1, grid=(), in_specs=[vmem] * len(parts), out_specs=vmem
        ),
        out_shape=jax.ShapeDtypeStruct(parts[0].shape, jnp.float32),
        compiler_params=pltpu.CompilerParams(vmem_limit_bytes=16 << 20),
        name="close",
    )(case, *(in_vmem(part) for part in parts))


LINE = {t: (((t ^ 1, t), (t ^ 3, t ^ 2)), ((t ^ 2, t),)) for t in range(4)}
X, Y = 1, 2


def is_traced(value):
    return not isinstance(value, int)


def exchange_plan(chips, runs):
    flat = lambda z, c, q: (2 * z + c) * runs + q
    across = lambda bit: [(q, q ^ bit) for q in range(runs)]
    cores = [(m, m ^ 1) for m in range(2 * chips)]

    def line(target, round_):
        return [
            (flat(s, c, q), flat(t, c, q))
            for c in range(2)
            for q in range(runs)
            for s, t in LINE[target(c, q)][round_]
        ]

    def corner(target, bit):
        return [
            (flat(target(c, q), c, q), flat(target(c, q), c, q ^ bit(c)))
            for c in range(2)
            for q in range(runs)
        ]

    def around(target, bit):
        return [
            (flat(s, c, q), flat(t, c, q ^ bit(c)))
            for c in range(2)
            for q in range(runs)
            for s, t in LINE[target(c, q)][1]
        ]

    step = lambda z, c, q: flat(z, c, q ^ (Y, X)[c])
    devices = [(z, c, q) for z in range(chips) for c in range(2) for q in range(runs)]
    straight = [(flat(z, c, q), step(z, c, q)) for z, c, q in devices]
    crosswise = [(flat(z, c, q), step(z, 1 - c, q)) for z, c, q in devices]
    return across, cores, line, corner, around, straight, crosswise


def on_square(snapshots, block_cols, mass_blocks):
    node_count, column_count = snapshots.shape
    blk = mass_blocks.shape[1]
    blocks_here = node_count // blk
    rim = HB * blk
    half = column_count // 2
    runs = lax.axis_size("run")
    chips = lax.axis_size("mesh") // 2
    both = ("mesh", "run")
    across, cores, line, corner, around, straight, crosswise = exchange_plan(chips, runs)
    shard = lax.axis_index("mesh")
    column = lax.axis_index("run")
    core, chip = shard % 2, shard // 2
    local_cols = block_cols - (shard * blocks_here - HB)

    def over_x(v):
        return lax.ppermute(v, "run", across(X))

    def over_y(v):
        return lax.ppermute(v, "run", across(Y))

    pick = core[None].astype(jnp.int32)
    shards = 2 * chips
    west, east = (0, half), (half, half)
    middle = (rim, node_count - 2 * rim)
    ends = (0, rim), (node_count - rim, rim)
    left_edge, right_edge = parts_of(
        snapshots, *(tuple((end, side) for end in ends) for side in (west, east))
    )
    a_edge = over_x(left_edge)
    b_edge = over_y(right_edge)
    left_middle, right_middle = parts_of(snapshots, ((middle, west),), ((middle, east),))
    a1 = over_x(left_middle)
    b2 = over_y(right_middle)
    last_rows, first_rows = rims_of(left_edge, right_edge, a_edge, b_edge)
    low = lax.ppermute(last_rows, "mesh", [(i, i + 1) for i in range(shards - 1)])
    high = lax.ppermute(first_rows, "mesh", [(i + 1, i) for i in range(shards - 1)])
    mine, others = sides_of(pick, snapshots)
    got = lax.ppermute(mine, both, straight)
    got_too = lax.ppermute(others, both, crosswise)

    top = rim + node_count
    all_rows, every = (0, rim), (0, column_count)

    def towards(core_a):
        return lambda c, q: q ^ jnp.where(c == core_a, X, Y) if is_traced(c) else q ^ (X, Y)[c != core_a]

    def crossing(core_a):
        return lambda c: (Y, X)[c != core_a]

    w, keep0, send0 = fused(
        local_cols, pick, mass_blocks, [low, in_hbm(snapshots), high],
        [
            (0, all_rows, every, 0, 0), (1, (0, node_count), every, rim, 0),
            (2, all_rows, every, top, 0),
        ],
    )
    beyond = (column_count, column_count)
    near_rows = [
        (piece, rows, (0, half), rim + to, lane)
        for edge, inner, lane in ((2, 3, 0), (4, 5, half))
        for piece, rows, to in (
            (edge, (0, rim), 0),
            (inner, (0, node_count - 2 * rim), rim),
            (edge, (rim, rim), node_count - rim),
        )
    ]
    wx, wx_side, rows = fused(
        local_cols, pick, mass_blocks, [low, high, a_edge, a1, b_edge, b2],
        [(0, all_rows, beyond, 0, 0), (1, all_rows, beyond, top, 0), *near_rows],
        multiplies=False, hands_out=True,
    )
    keep1, send1 = products_of_rows(pick, rows, rim, w, wx)
    w_too = lax.ppermute(w, "mesh", cores)
    wx_too = lax.ppermute(wx_side, "mesh", cores)
    total2, coded2 = chip_products(pick, got, got_too, w, w_too, wx, wx_too)
    own_target = lambda c, q: q
    came = lax.ppermute(send0, "mesh", cores)
    own, coded = merge(keep0, came)
    came = lax.ppermute(coded, both, line(own_target, 0))
    own, coded = merge(own, came, step_body)
    own_came = lax.ppermute(coded, both, line(own_target, 1))

    def added(kept, sent):
        came = lax.ppermute(sent, "mesh", cores)
        return merge(kept, came)

    def finished(total, coded, core_a):
        target, bit = towards(core_a), crossing(core_a)
        came = lax.ppermute(coded, both, line(target, 0))
        at_target = (chip == target(core, column))[None].astype(jnp.int32)
        near, leg, far = turn(at_target, total, came, column_count)
        leg = lax.ppermute(leg, both, line(target, 1) + corner(target, bit))
        far = lax.ppermute(far, both, around(target, bit))
        return near, leg, far

    stage1 = finished(*added(keep1, send1), 0)
    stage2 = finished(total2, coded2, 1)
    near = jnp.where((chip == (column ^ X)) == (core == 0), 1, 2)
    case = jnp.where(chip == column, 0, jnp.where(chip == (column ^ (X | Y)), 3 + core, near))
    return close(case[None].astype(jnp.int32), own, own_came, *stage1, *stage2)


def on_device(snapshots, block_cols, mass_blocks):
    node_count, column_count = snapshots.shape
    blk = mass_blocks.shape[1]
    blocks_here = node_count // blk
    rim = HB * blk
    shards = lax.axis_size("mesh")
    low = lax.ppermute(snapshots[-rim:], "mesh", [(i, i + 1) for i in range(shards - 1)])
    high = lax.ppermute(snapshots[:rim], "mesh", [(i + 1, i) for i in range(shards - 1)])
    local_cols = block_cols - (lax.axis_index("mesh") * blocks_here - HB)
    (weighted,) = fused(
        local_cols, jnp.zeros((1,), jnp.int32), mass_blocks, [low, snapshots, high],
        [
            (0, (0, rim), (0, column_count), 0, 0),
            (1, (0, node_count), (0, column_count), rim, 0),
            (2, (0, rim), (0, column_count), rim + node_count, 0),
        ],
        multiplies=False,
    )
    gathered = lax.all_gather(snapshots, "run", axis=1, tiled=True)
    return lax.psum_scatter(
        contract_nodes(gathered, weighted), "mesh", scatter_dimension=0, tiled=True
    )


def solution(mesh):
    placed = (P("mesh", "run"), P("mesh", None), P("mesh", None, None))
    square = mesh.shape["run"] == 4 and mesh.shape["mesh"] == 8

    def body(*args):
        return (on_square if square else on_device)(*args)

    return jax.shard_map(
        body, mesh=mesh, in_specs=placed, out_specs=P("mesh", "run"), check_vma=False
    )
```

```python
import functools

import jax
import jax.numpy as jnp
from jax import lax
from jax.experimental import pallas as pl
from jax.experimental.pallas import tpu as pltpu
from jax.sharding import PartitionSpec as P


HB = 2


def contract_nodes(left_cols, right_cols):
    return lax.dot_general(
        left_cols, right_cols, (((0,), (0,)), ((), ())), preferred_element_type=jnp.float32
    )


def span(start, size):
    return slice(start, start + size)


def fused_body(plan, *refs):
    refs = list(refs)
    cols_ref, pick_ref = refs.pop(0), refs.pop(0)
    mass_hbm = refs.pop(0)
    pieces = [refs.pop(0) for _ in range(plan["count"])]
    made_ref = refs.pop(0)
    keep_ref, send_ref = (refs.pop(0), refs.pop(0)) if plan["multiplies"] else (None, None)
    side_ref = refs.pop(0) if plan["hands_out"] else None
    rows_ref = refs.pop(0)
    mass_ref = refs.pop(0)
    sems = refs.pop(0)
    blk, rim, half = plan["blk"], plan["rim"], plan["half"]

    used = iter(range(64))
    fetch = lambda source, target: pltpu.make_async_copy(source, target, sems.at[next(used)])

    def place(to, size):
        if isinstance(to, int):
            return span(to, size)
        return pl.ds(pl.multiple_of(to[0] + pick_ref[0] * (to[1] - to[0]), size), size)

    rows_in = [
        fetch(pieces[p].at[span(r, n), span(c, w)], rows_ref.at[place(to, n), span(lane, w)])
        for p, (r, n), (c, w), to, lane in plan["places"]
    ]
    mass_in, parts = [], plan["parts"]
    size = mass_ref.shape[0] // parts
    for i in range(parts):
        part = span(i * size, size)
        mass_in.append(fetch(mass_hbm.at[part], mass_ref.at[part]))
    for copy in rows_in + mass_in:
        copy.start()
    for copy in rows_in:
        copy.wait()

    for row in range(mass_ref.shape[0]):
        if row % size == 0:
            mass_in[row // size].wait()
        picked = jnp.concatenate(
            [
                rows_ref[pl.ds(pl.multiple_of(cols_ref[k, row] * blk, blk), blk), :]
                for k in range(cols_ref.shape[0])
            ],
            axis=0,
        )
        product = jnp.dot(mass_ref[row], picked, preferred_element_type=jnp.float32)
        made_ref[row * blk : (row + 1) * blk, :] = product.astype(made_ref.dtype)

    if plan["hands_out"]:
        side_ref[...] = made_ref[:, pl.ds(pl.multiple_of((1 - pick_ref[0]) * half, half), half)]
    if plan["multiplies"]:
        own, nodes = made_ref.shape[1], made_ref.shape[0]
        for target, first in ((keep_ref, pick_ref[0]), (send_ref, 1 - pick_ref[0])):
            left = rows_ref[span(rim, nodes), pl.ds(pl.multiple_of(first * half, half), half)]
            target[:, :own] = contract_nodes(left, made_ref[...])


def in_hbm(array):
    return pltpu.with_memory_space_constraint(array, pltpu.HBM)


def parts_body(cuts, source, *refs):
    targets, sems = refs[:-1], refs[-1]
    copies = []
    for pieces, target in zip(cuts, targets):
        done = 0
        for (r, n), (c, w) in pieces:
            copies.append(
                pltpu.make_async_copy(
                    source.at[span(r, n), span(c, w)],
                    target.at[span(done, n), :],
                    sems.at[len(copies)],
                )
            )
            done += n
    for copy in copies:
        copy.start()
    for copy in copies:
        copy.wait()


def parts_of(array, *cuts):
    shapes = [(sum(n for (_, n), _ in pieces), pieces[0][1][1]) for pieces in cuts]
    return pl.pallas_call(
        functools.partial(parts_body, cuts),
        in_specs=[pl.BlockSpec(memory_space=pl.ANY)],
        out_specs=[pl.BlockSpec(memory_space=pltpu.VMEM)] * len(cuts),
        out_shape=[pltpu.VMEM(shape, array.dtype) for shape in shapes],
        scratch_shapes=[pltpu.SemaphoreType.DMA((sum(len(pieces) for pieces in cuts),))],
        compiler_params=pltpu.CompilerParams(vmem_limit_bytes=4 << 20),
    )(in_hbm(array))


def sides_body(pick_ref, source, first_ref, second_ref, sems):
    half = first_ref.shape[1]
    copies = []
    for target, side in ((first_ref, pick_ref[0]), (second_ref, 1 - pick_ref[0])):
        piece = source.at[:, pl.ds(pl.multiple_of(side * half, half), half)]
        copies.append(pltpu.make_async_copy(piece, target, sems.at[len(copies)]))
    for copy in copies:
        copy.start()
    for copy in copies:
        copy.wait()


def sides_of(pick, array):
    nodes, width = array.shape
    return pl.pallas_call(
        sides_body,
        grid_spec=pltpu.PrefetchScalarGridSpec(
            num_scalar_prefetch=1,
            grid=(),
            in_specs=[pl.BlockSpec(memory_space=pl.ANY)],
            out_specs=[pl.BlockSpec(memory_space=pltpu.VMEM)] * 2,
            scratch_shapes=[pltpu.SemaphoreType.DMA((2,))],
        ),
        out_shape=[pltpu.VMEM((nodes, width // 2), array.dtype)] * 2,
        compiler_params=pltpu.CompilerParams(vmem_limit_bytes=4 << 20),
    )(pick, in_hbm(array))


def rims_body(pick_ref, *refs):
    edges, targets = refs[:-2], refs[-2:]
    rim = targets[0].shape[0]
    for target, side in zip(targets, (1 - pick_ref[0], pick_ref[0])):
        rows = pl.ds(pl.multiple_of(side * rim, rim), rim)
        for i, edge in enumerate(edges):
            target[:, span(i * edge.shape[1], edge.shape[1])] = edge[rows, :]


def rims_of(pick, *edges):
    vmem = pl.BlockSpec(memory_space=pltpu.VMEM)
    shape = (edges[0].shape[0] // 2, sum(edge.shape[1] for edge in edges))
    return pl.pallas_call(
        rims_body,
        grid_spec=pltpu.PrefetchScalarGridSpec(
            num_scalar_prefetch=1, grid=(), in_specs=[vmem] * len(edges), out_specs=[vmem] * 2
        ),
        out_shape=[pltpu.VMEM(shape, edges[0].dtype)] * 2,
        compiler_params=pltpu.CompilerParams(vmem_limit_bytes=4 << 20),
        name="rims",
    )(pick, *(in_vmem(edge) for edge in edges))


def in_vmem(array):
    return pltpu.with_memory_space_constraint(array, pltpu.VMEM)


def fused(local_cols, pick, mass_blocks, pieces, places, multiplies=True, hands_out=False):
    block_rows, blk, stored = mass_blocks.shape
    rim = HB * blk
    nodes = block_rows * blk
    width = max(lane + w for _, _, (_, w), _, lane in places)
    half = width // 2
    row_count = max(n + (to if isinstance(to, int) else max(to)) for _, (_, n), _, to, _ in places)
    parts = 4 if block_rows % 4 == 0 else 1
    plan = dict(
        blk=blk, rim=rim, half=half, multiplies=multiplies, places=places, count=len(pieces),
        parts=parts, hands_out=hands_out,
    )
    operands = [in_hbm(mass_blocks), *pieces]
    specs = [pl.BlockSpec(memory_space=pl.ANY)] * len(operands)
    outs = [pltpu.VMEM((nodes, width), jnp.bfloat16)]
    flops = 8 * nodes * stored * width
    if multiplies:
        outs += [pltpu.VMEM((half, width), jnp.float32)] * 2
        flops += 4 * nodes * half * width
    rows = [pltpu.VMEM((row_count, width), jnp.bfloat16)]
    side = [pltpu.VMEM((nodes, half), jnp.bfloat16)]
    outs, scratch = (outs + side + rows, []) if hands_out else (outs, rows)
    return pl.pallas_call(
        functools.partial(fused_body, plan),
        grid_spec=pltpu.PrefetchScalarGridSpec(
            num_scalar_prefetch=2,
            grid=(),
            in_specs=specs,
            out_specs=[pl.BlockSpec(memory_space=pltpu.VMEM)] * len(outs),
            scratch_shapes=[
                *scratch,
                pltpu.VMEM(mass_blocks.shape, jnp.bfloat16),
                pltpu.SemaphoreType.DMA((len(places) + parts,)),
            ],
        ),
        out_shape=outs,
        cost_estimate=pl.CostEstimate(flops=flops, bytes_accessed=8 << 20, transcendentals=0),
        compiler_params=pltpu.CompilerParams(vmem_limit_bytes=24 << 20),
    )(local_cols.T, pick, *operands)


def products_of_rows_body(rim, pick_ref, rows_ref, w_ref, x_ref, keep_ref, send_ref):
    own, nodes, half = w_ref.shape[1], w_ref.shape[0], x_ref.shape[1] // 2
    for target, first in ((keep_ref, pick_ref[0]), (send_ref, 1 - pick_ref[0])):
        left = rows_ref[span(rim, nodes), pl.ds(pl.multiple_of(first * half, half), half)]
        target[:, :own] = contract_nodes(left, w_ref[...])
        right = x_ref[:, pl.ds(pl.multiple_of((1 - first) * half, half), half)]
        target[:, own:] = contract_nodes(left, right)


def products_of_rows(pick, rows, rim, w, x):
    nodes, own = w.shape
    half = x.shape[1] // 2
    vmem = pl.BlockSpec(memory_space=pltpu.VMEM)
    return pl.pallas_call(
        functools.partial(products_of_rows_body, rim),
        grid_spec=pltpu.PrefetchScalarGridSpec(
            num_scalar_prefetch=1, grid=(), in_specs=[vmem] * 3, out_specs=[vmem] * 2
        ),
        out_shape=[pltpu.VMEM((half, own + half), jnp.float32)] * 2,
        cost_estimate=pl.CostEstimate(
            flops=4 * nodes * half * (own + half), bytes_accessed=8 << 20, transcendentals=0
        ),
        compiler_params=pltpu.CompilerParams(vmem_limit_bytes=16 << 20),
    )(pick, *(in_vmem(array) for array in (rows, w, x)))


TOP = 32000.0
EXTRA = 16


def encoded(values):
    peak = jnp.maximum(jnp.max(jnp.abs(values), axis=0, keepdims=True), 1e-30)
    power = jnp.ceil(jnp.log2(peak))
    whole = jnp.round(values * (jnp.exp2(-power) * TOP)).astype(jnp.int32)
    return whole.astype(jnp.int16), power.astype(jnp.int32)


def put_encoded(target, values):
    rows, width = values.shape
    whole, power = encoded(values)
    target[:rows, :] = whole
    target[rows:, :] = jnp.broadcast_to(power, (EXTRA, width)).astype(jnp.int16)


def decoded(source, lo, hi):
    rows = source.shape[0] - EXTRA
    power = source[rows:, lo:hi].astype(jnp.int32).astype(jnp.float32)[:1]
    whole = source[:rows, lo:hi].astype(jnp.int32).astype(jnp.float32)
    return whole * (jnp.exp2(power) * (1.0 / TOP))


def merge_body(kept_ref, came_ref, total_ref, coded_ref):
    total = kept_ref[...] + came_ref[...]
    total_ref[...] = total
    put_encoded(coded_ref, total)


def merge(kept, came, body=merge_body):
    rows, width = kept.shape
    vmem = pl.BlockSpec(memory_space=pltpu.VMEM)
    return pl.pallas_call(
        body,
        in_specs=[vmem] * 2,
        out_specs=[vmem] * 2,
        out_shape=[
            pltpu.VMEM((rows, width), jnp.float32),
            pltpu.VMEM((rows + EXTRA, width), jnp.int16),
        ],
        cost_estimate=pl.CostEstimate(
            flops=8 * rows * width, bytes_accessed=14 * rows * width, transcendentals=0
        ),
        compiler_params=pltpu.CompilerParams(vmem_limit_bytes=16 << 20),
    )(in_vmem(kept), in_vmem(came))


def step_body(total_ref, came_ref, next_ref, coded_ref):
    total = total_ref[...] + decoded(came_ref, 0, total_ref.shape[1])
    next_ref[...] = total
    put_encoded(coded_ref, total)


def chip_body(pick_ref, left, left_too, w, w_too, x, x_too, total_ref, coded_ref):
    own, half = w.shape[1], x_too.shape[1]
    side = x[:, pl.ds(pl.multiple_of(pick_ref[0] * half, half), half)]
    near = contract_nodes(left[...], w[...]) + contract_nodes(left_too[...], w_too[...])
    total_ref[:, :own] = near
    total_ref[:, own:] = contract_nodes(left[...], side) + contract_nodes(left_too[...], x_too[...])
    put_encoded(coded_ref, total_ref[...])


def chip_products(pick, *operands):
    left, _, w, _, _, x_too = operands
    nodes, rows = left.shape
    total = w.shape[1] + x_too.shape[1]
    vmem = pl.BlockSpec(memory_space=pltpu.VMEM)
    return pl.pallas_call(
        chip_body,
        grid_spec=pltpu.PrefetchScalarGridSpec(
            num_scalar_prefetch=1, grid=(), in_specs=[vmem] * 6, out_specs=[vmem] * 2
        ),
        out_shape=[
            pltpu.VMEM((rows, total), jnp.float32),
            pltpu.VMEM((rows + EXTRA, total), jnp.int16),
        ],
        cost_estimate=pl.CostEstimate(
            flops=4 * nodes * rows * total, bytes_accessed=8 << 20, transcendentals=0
        ),
        compiler_params=pltpu.CompilerParams(vmem_limit_bytes=16 << 20),
    )(pick, *(in_vmem(operand) for operand in operands))


def turn_body(own, flag_ref, total_ref, came_ref, near_ref, leg_ref, far_ref, coded_ref):
    width = total_ref.shape[1]
    total = total_ref[...] + decoded(came_ref, 0, width)
    near_ref[...] = total[:, :own]
    put_encoded(coded_ref, total)
    far_ref[...] = coded_ref[:, own:]
    half = width - own
    first = pl.multiple_of(flag_ref[0] * half, half)
    leg_ref[...] = coded_ref[:, pl.ds(first, own)]


def turn(flag, total, came, own):
    rows, width = total.shape
    coded = lambda columns: pltpu.VMEM((rows + EXTRA, columns), jnp.int16)
    vmem = pl.BlockSpec(memory_space=pltpu.VMEM)
    return pl.pallas_call(
        functools.partial(turn_body, own),
        grid_spec=pltpu.PrefetchScalarGridSpec(
            num_scalar_prefetch=1,
            grid=(),
            in_specs=[vmem] * 2,
            out_specs=[vmem] * 3,
            scratch_shapes=[pltpu.VMEM((rows + EXTRA, width), jnp.int16)],
        ),
        out_shape=[pltpu.VMEM((rows, own), jnp.float32), coded(own), coded(width - own)],
        cost_estimate=pl.CostEstimate(
            flops=8 * rows * width, bytes_accessed=12 * rows * width, transcendentals=0
        ),
        compiler_params=pltpu.CompilerParams(vmem_limit_bytes=16 << 20),
    )(flag, in_vmem(total), in_vmem(came))


def close_body(case_ref, own, own_came, near1, leg1, far1, near2, leg2, far2, out_ref):
    width = out_ref.shape[1]
    half = width // 2
    case = case_ref[0]

    @pl.when(case == 0)
    def _():
        out_ref[...] = own[...] + decoded(own_came, 0, width)

    for number, near, leg in ((1, near1, leg1), (2, near2, leg2)):

        @pl.when(case == number)
        def _():
            out_ref[...] = near[...] + decoded(leg, 0, width)

    first, second = (leg1, far1), (leg2, far2)
    for number, pair in ((3, (second, first)), (4, (first, second))):

        @pl.when(case == number)
        def _():
            for i, (leg, far) in enumerate(pair):
                out_ref[:, i * half : (i + 1) * half] = decoded(leg, half, width) + decoded(far, 0, half)


def close(case, *parts):
    vmem = pl.BlockSpec(memory_space=pltpu.VMEM)
    return pl.pallas_call(
        close_body,
        grid_spec=pltpu.PrefetchScalarGridSpec(
            num_scalar_prefetch=1, grid=(), in_specs=[vmem] * len(parts), out_specs=vmem
        ),
        out_shape=jax.ShapeDtypeStruct(parts[0].shape, jnp.float32),
        compiler_params=pltpu.CompilerParams(vmem_limit_bytes=16 << 20),
        name="close",
    )(case, *(in_vmem(part) for part in parts))


LINE = {t: (((t ^ 1, t), (t ^ 3, t ^ 2)), ((t ^ 2, t),)) for t in range(4)}
X, Y = 1, 2


def is_traced(value):
    return not isinstance(value, int)


def exchange_plan(chips, runs):
    flat = lambda z, c, q: (2 * z + c) * runs + q
    across = lambda bit: [(q, q ^ bit) for q in range(runs)]
    cores = [(m, m ^ 1) for m in range(2 * chips)]

    def line(target, round_):
        return [
            (flat(s, c, q), flat(t, c, q))
            for c in range(2)
            for q in range(runs)
            for s, t in LINE[target(c, q)][round_]
        ]

    def corner(target, bit):
        return [
            (flat(target(c, q), c, q), flat(target(c, q), c, q ^ bit(c)))
            for c in range(2)
            for q in range(runs)
        ]

    def around(target, bit):
        return [
            (flat(s, c, q), flat(t, c, q ^ bit(c)))
            for c in range(2)
            for q in range(runs)
            for s, t in LINE[target(c, q)][1]
        ]

    step = lambda z, c, q: flat(z, c, q ^ (Y, X)[c])
    devices = [(z, c, q) for z in range(chips) for c in range(2) for q in range(runs)]
    straight = [(flat(z, c, q), step(z, c, q)) for z, c, q in devices]
    crosswise = [(flat(z, c, q), step(z, 1 - c, q)) for z, c, q in devices]
    return across, cores, line, corner, around, straight, crosswise


def on_square(snapshots, block_cols, mass_blocks):
    node_count, column_count = snapshots.shape
    blk = mass_blocks.shape[1]
    blocks_here = node_count // blk
    rim = HB * blk
    half = column_count // 2
    runs = lax.axis_size("run")
    chips = lax.axis_size("mesh") // 2
    both = ("mesh", "run")
    across, cores, line, corner, around, straight, crosswise = exchange_plan(chips, runs)
    shard = lax.axis_index("mesh")
    column = lax.axis_index("run")
    core, chip = shard % 2, shard // 2
    local_cols = block_cols - (shard * blocks_here - HB)

    def over_x(v):
        return lax.ppermute(v, "run", across(X))

    def over_y(v):
        return lax.ppermute(v, "run", across(Y))

    pick = core[None].astype(jnp.int32)
    facing = [(m, m + (1 if m % 2 else -1)) for m in range(1, 2 * chips - 1)]
    west, east = (0, half), (half, half)
    middle = (rim, node_count - 2 * rim)
    ends = (0, rim), (node_count - rim, rim)
    left_edge, right_edge = parts_of(
        snapshots, *(tuple((end, side) for end in ends) for side in (west, east))
    )
    a_edge = over_x(left_edge)
    b_edge = over_y(right_edge)
    left_middle, right_middle = parts_of(snapshots, ((middle, west),), ((middle, east),))
    a1 = over_x(left_middle)
    b2 = over_y(right_middle)
    inner_rows, outer_rows = rims_of(pick, left_edge, right_edge, a_edge, b_edge)
    outer = lax.ppermute(outer_rows, "mesh", facing)
    inner = lax.ppermute(inner_rows, "mesh", cores)
    mine, others = sides_of(pick, snapshots)
    got = lax.ppermute(mine, both, straight)
    got_too = lax.ppermute(others, both, crosswise)

    top = rim + node_count
    all_rows, every = (0, rim), (0, column_count)

    def towards(core_a):
        return lambda c, q: q ^ jnp.where(c == core_a, X, Y) if is_traced(c) else q ^ (X, Y)[c != core_a]

    def crossing(core_a):
        return lambda c: (Y, X)[c != core_a]

    w, keep0, send0 = fused(
        local_cols, pick, mass_blocks, [inner, in_hbm(snapshots), outer],
        [
            (0, all_rows, every, (top, 0), 0), (1, (0, node_count), every, rim, 0),
            (2, all_rows, every, (0, top), 0),
        ],
    )
    beyond = (column_count, column_count)
    near_rows = [
        (piece, rows, (0, half), rim + to, lane)
        for edge, inner, lane in ((2, 3, 0), (4, 5, half))
        for piece, rows, to in (
            (edge, (0, rim), 0),
            (inner, (0, node_count - 2 * rim), rim),
            (edge, (rim, rim), node_count - rim),
        )
    ]
    wx, wx_side, rows = fused(
        local_cols, pick, mass_blocks, [inner, outer, a_edge, a1, b_edge, b2],
        [(0, all_rows, beyond, (top, 0), 0), (1, all_rows, beyond, (0, top), 0), *near_rows],
        multiplies=False, hands_out=True,
    )
    keep1, send1 = products_of_rows(pick, rows, rim, w, wx)
    w_too = lax.ppermute(w, "mesh", cores)
    wx_too = lax.ppermute(wx_side, "mesh", cores)
    total2, coded2 = chip_products(pick, got, got_too, w, w_too, wx, wx_too)
    own_target = lambda c, q: q
    came = lax.ppermute(send0, "mesh", cores)
    own, coded = merge(keep0, came)
    came = lax.ppermute(coded, both, line(own_target, 0))
    own, coded = merge(own, came, step_body)
    own_came = lax.ppermute(coded, both, line(own_target, 1))

    def added(kept, sent):
        came = lax.ppermute(sent, "mesh", cores)
        return merge(kept, came)

    def finished(total, coded, core_a):
        target, bit = towards(core_a), crossing(core_a)
        came = lax.ppermute(coded, both, line(target, 0))
        at_target = (chip == target(core, column))[None].astype(jnp.int32)
        near, leg, far = turn(at_target, total, came, column_count)
        leg = lax.ppermute(leg, both, line(target, 1) + corner(target, bit))
        far = lax.ppermute(far, both, around(target, bit))
        return near, leg, far

    stage1 = finished(*added(keep1, send1), 0)
    stage2 = finished(total2, coded2, 1)
    near = jnp.where((chip == (column ^ X)) == (core == 0), 1, 2)
    case = jnp.where(chip == column, 0, jnp.where(chip == (column ^ (X | Y)), 3 + core, near))
    return close(case[None].astype(jnp.int32), own, own_came, *stage1, *stage2)


def on_device(snapshots, block_cols, mass_blocks):
    node_count, column_count = snapshots.shape
    blk = mass_blocks.shape[1]
    blocks_here = node_count // blk
    rim = HB * blk
    shards = lax.axis_size("mesh")
    low = lax.ppermute(snapshots[-rim:], "mesh", [(i, i + 1) for i in range(shards - 1)])
    high = lax.ppermute(snapshots[:rim], "mesh", [(i + 1, i) for i in range(shards - 1)])
    local_cols = block_cols - (lax.axis_index("mesh") * blocks_here - HB)
    (weighted,) = fused(
        local_cols, jnp.zeros((1,), jnp.int32), mass_blocks, [low, snapshots, high],
        [
            (0, (0, rim), (0, column_count), 0, 0),
            (1, (0, node_count), (0, column_count), rim, 0),
            (2, (0, rim), (0, column_count), rim + node_count, 0),
        ],
        multiplies=False,
    )
    gathered = lax.all_gather(snapshots, "run", axis=1, tiled=True)
    return lax.psum_scatter(
        contract_nodes(gathered, weighted), "mesh", scatter_dimension=0, tiled=True
    )


def solution(mesh):
    placed = (P("mesh", "run"), P("mesh", None), P("mesh", None, None))
    square = mesh.shape["run"] == 4 and mesh.shape["mesh"] == 8

    def body(*args):
        return (on_square if square else on_device)(*args)

    return jax.shard_map(
        body, mesh=mesh, in_specs=placed, out_specs=P("mesh", "run"), check_vma=False
    )
```
